128 devices in a mesh: gx: 16 (over x, z), gy: 8 (over y, core).
Axes of the slice: x: 4, y: 4, z: 4, core: 2. Of those that a mesh axis runs over, the one named last changes fastest.
Arguments:
- reference_scan: bfloat16 [256, 256, 2048], P('gx', 'gy'), may hold values from -6 to 6
- ref_gradient: bfloat16 [3, 256, 256, 2048], P(None, 'gx', 'gy'), may hold values from -6 to 6
- deformed_scan: bfloat16 [256, 256, 2048], P('gx', 'gy'), may hold values from -6 to 6
- interp_weights: bfloat16 [256, 256, 2048], P('gx', 'gy'), may hold values from 0 to 1
- sample_mask: int32 [256, 256, 2048], P('gx', 'gy'), may hold values from 0 to 1, as said below
- block_list: int32 [16, 32768], P('gx', 'gy'), may hold values from -1 to 8191, as said below
- offsets: int32 [2, 256, 256, 4], P(None, 'gx', 'gy'), may hold values from -4 to 4, as said below
Outputs:
- increment: float32 [3, 256, 256, 5], P(None, 'gx', 'gy')
- cg_residual: float32 [3, 256, 256, 5], P(None, 'gx', 'gy')
The draws below stay inside these ranges and needn't reach their ends.
Inputs may be any that keep to these rules, and one draw needn't show every extreme that they name: sample_mask is 0 in every block of 128 voxels that its device's block_list does not name. `block_list`: each device's 4096 entries are first distinct local block indices, then -1 to the end; some device names exactly 4096 blocks. `offsets`: both ends of the range occur.
All inputs are finite; a program needn't handle non-finite values.
Results may differ from the reference program's by a relative error of at most 0.0045.
Values may be sent and summed in bfloat16 or wider, within the bound.
No kernel may reach another device: no remote copies, remote signals or barrier semaphores. Data moves between devices by JAX's collectives and lax.ppermute only.
A program may use at most 320 MiB of HBM per device.

```python
import jax
import jax.numpy as jnp
from jax import lax

EX = 16
EY = 32
EZ = 4
BOUND = 4
ITERS = 3
CAP = 4096
NEX = 256
NEY = 256
N_GX = 16
N_GY = 8


def live_blocks(key):
    base = jax.random.fold_in(key, 4021)
    split_keys = jax.random.split(base, 4)
    devices_total = N_GX * N_GY
    local_blocks = EX * EY * EZ * 4
    counts = jax.random.randint(split_keys[0], (devices_total,), CAP // 8, CAP + 1)
    busiest = jax.random.randint(split_keys[1], (), 0, devices_total)
    counts = jnp.where(jnp.arange(devices_total) == busiest, CAP, counts)
    orders = jax.vmap(lambda inner: jax.random.permutation(inner, local_blocks))(jax.random.split(split_keys[2], devices_total))
    ranks = jnp.argsort(orders, axis=1)
    listed = (ranks < counts[:, None]).astype(jnp.int32)
    chosen = jnp.where(jnp.arange(CAP)[None, :] < counts[:, None], orders[:, :CAP], -1)
    voxels = (jax.random.randint(split_keys[3], (devices_total, local_blocks, 128), 0, 10) < 6).astype(jnp.int32)
    voxels = voxels * listed[:, :, None]
    return (chosen.astype(jnp.int32), voxels)


def draw_sample_mask(key, part):
    chosen, voxels = live_blocks(key)
    grid = jnp.transpose(voxels.reshape(N_GX, N_GY, EX, EY, EZ * 512), (0, 2, 1, 3, 4))
    return grid.reshape(EX * N_GX, EY * N_GY, EZ * 512).astype(jnp.int32)


def draw_block_list(key, part):
    chosen, voxels = live_blocks(key)
    return chosen.reshape(N_GX, N_GY * CAP).astype(jnp.int32)


def draw_offsets(key, part):
    inner = jax.random.fold_in(key, 733)
    values = jax.random.randint(inner, (2, EX * N_GX, EY * N_GY, EZ), -BOUND, BOUND + 1)
    values = values.at[:, 0, 0, 0].set(BOUND)
    values = values.at[:, EX * N_GX - 1, EY * N_GY - 1, EZ - 1].set(-BOUND)
    return values.astype(jnp.int32)


def shard_levels(rng, extent, shards, smallest, top_value):
    level, own = 1.0, jax.random.fold_in(rng, 6)
    for dim, blocks in shards:
        heights = jnp.exp(jax.random.uniform(jax.random.fold_in(own, dim), (blocks,), jnp.float32, smallest / len(shards), top_value / len(shards)))
        level = level * jnp.repeat(heights, extent[dim] // blocks).reshape([-1 if axis == dim else 1 for axis in range(len(extent))])
    return level


def gaussian(stream_key, shape, width, limit, cuts=(), kind=jnp.bfloat16):
    result = jax.random.normal(stream_key, shape, jnp.float32) * width
    if len(cuts) > 0:
        result = shard_levels(stream_key, shape, cuts, -0.22, 0.18) * result
    return jnp.clip(result, min=-limit, max=limit).astype(kind)


def setup_inputs(seed: int = 0) -> dict:
    key_list = jax.random.split(jax.random.key(seed), 8)
    return {
        "reference_scan": gaussian(key_list[0], (NEX, NEY, EZ * 512), 1.0, 6.0, ((0, 16), (1, 8))),
        "ref_gradient": gaussian(key_list[1], (3, NEX, NEY, EZ * 512), 1.0, 6.0, ((1, 16), (2, 8))),
        "deformed_scan": gaussian(key_list[2], (NEX, NEY, EZ * 512), 1.0, 6.0, ((0, 16), (1, 8))),
        "interp_weights": jnp.clip(1.0 * jax.random.uniform(key_list[3], (NEX, NEY, EZ * 512), jnp.float32) ** shard_levels(key_list[3], (NEX, NEY, EZ * 512), ((0, 16), (1, 8)), -0.2, 0.2), 0.0, 1.0).astype(jnp.bfloat16),
        "sample_mask": draw_sample_mask(jax.random.fold_in(key_list[7], 71), 0),
        "block_list": draw_block_list(jax.random.fold_in(key_list[7], 71), 0),
        "offsets": draw_offsets(jax.random.fold_in(key_list[7], 71), 0),
    }


tikhonov = 8.0


def shape_table():
    voxel = jnp.arange(512)
    coords = [((voxel // 64).astype(jnp.float32) + 0.5) / 8.0, (((voxel // 8) % 8).astype(jnp.float32) + 0.5) / 8.0, ((voxel % 8).astype(jnp.float32) + 0.5) / 8.0]
    rows = []
    for node in range(8):
        bits = [(node >> 2) & 1, (node >> 1) & 1, node & 1]
        value = jnp.ones((512,), jnp.float32)
        for axis_pos in range(3):
            value = value * (coords[axis_pos] if bits[axis_pos] else 1.0 - coords[axis_pos])
        rows.append(value)
    return jnp.transpose(jnp.stack(rows).reshape(8, 4, 128), (1, 0, 2))


def reference(reference_scan, ref_gradient, deformed_scan, interp_weights, sample_mask, block_list, offsets):
    margin = BOUND + 1
    total_x = EX * N_GX
    total_y = EY * N_GY
    padded = jnp.pad(deformed_scan, ((margin, margin), (margin, margin), (0, 0)))
    span_y = total_y + 2 * margin
    flat_scan = padded.reshape(-1, EZ, 512)
    pos_x = jnp.arange(total_x)[:, None, None]
    pos_y = jnp.arange(total_y)[None, :, None]
    source = (pos_x + offsets[0] + margin) * span_y + pos_y + offsets[1] + margin
    layer = jnp.broadcast_to(jnp.arange(EZ)[None, None, :], source.shape)
    near = flat_scan[source, layer].astype(jnp.float32)
    far = flat_scan[source + span_y, layer].astype(jnp.float32)
    weights = interp_weights.reshape(total_x, total_y, EZ, 512).astype(jnp.float32)
    warped = weights * near + (1.0 - weights) * far
    residual_image = (reference_scan.reshape(total_x, total_y, EZ, 512).astype(jnp.float32) - warped).astype(jnp.bfloat16)
    devices_total = N_GX * N_GY
    local_blocks = EX * EY * EZ * 4
    elements = EX * EY * EZ

    def to_devices(array):
        moved = jnp.transpose(array.reshape(N_GX, EX, N_GY, EY, EZ * 512), (0, 2, 1, 3, 4))
        return moved.reshape(devices_total, local_blocks, 128)

    resid_dev = to_devices(residual_image.reshape(total_x, total_y, EZ * 512))
    mask_dev = to_devices(sample_mask)
    grad_dev = jnp.stack([to_devices(ref_gradient[comp]) for comp in range(3)], axis=1)
    lists = block_list.reshape(devices_total, CAP)
    table = shape_table()

    def per_device(parts):
        grads, resid, mask, entries = parts
        listed = entries >= 0
        safe = jnp.maximum(entries, 0)
        shapes = table[safe % 4]
        grad_rows = jnp.moveaxis(grads[:, safe], 0, 1).astype(jnp.float32)
        product = (shapes[:, :, None, :] * grad_rows[:, None, :, :]).reshape(CAP, 24, 128)
        jacobian = lax.optimization_barrier(product.astype(jnp.bfloat16)).astype(jnp.float32)
        sampled = mask[safe].astype(jnp.float32) * listed[:, None].astype(jnp.float32)
        weighted = jacobian * sampled[:, None, :]
        hessian = jnp.einsum("bdv,bev->bde", weighted, jacobian, precision=lax.Precision.HIGHEST)
        gradient = jnp.einsum("bdv,bv->bd", weighted, resid[safe].astype(jnp.float32), precision=lax.Precision.HIGHEST)
        elem_hess = jnp.zeros((elements, 24, 24), jnp.float32).at[safe // 4].add(hessian)
        elem_load = jnp.zeros((elements, 24), jnp.float32).at[safe // 4].add(gradient)
        return elem_hess, elem_load

    elem_hess, elem_load = lax.map(per_device, (grad_dev, resid_dev, mask_dev, lists))
    stiffness = jnp.transpose(elem_hess.reshape(N_GX, N_GY, EX, EY, EZ, 24, 24), (0, 2, 1, 3, 4, 5, 6)).reshape(total_x, total_y, EZ, 24, 24)
    loads = jnp.transpose(elem_load.reshape(N_GX, N_GY, EX, EY, EZ, 24), (0, 2, 1, 3, 4, 5)).reshape(total_x, total_y, EZ, 24)

    def spread(field):
        wide = jnp.pad(field, ((0, 0), (0, 1), (0, 1), (0, 0)))
        pieces = []
        for node in range(8):
            i_bit, j_bit, l_bit = (node >> 2) & 1, (node >> 1) & 1, node & 1
            pieces.append(wide[:, i_bit:i_bit + total_x, j_bit:j_bit + total_y, l_bit:l_bit + EZ])
        stacked = jnp.stack(pieces)
        return jnp.transpose(stacked, (2, 3, 4, 0, 1)).reshape(total_x, total_y, EZ, 24)

    def collect(values):
        parts = jnp.transpose(values.reshape(total_x, total_y, EZ, 8, 3), (3, 4, 0, 1, 2))
        total = jnp.zeros((3, total_x + 1, total_y + 1, EZ + 1), jnp.float32)
        for node in range(8):
            i_bit, j_bit, l_bit = (node >> 2) & 1, (node >> 1) & 1, node & 1
            total = total + jnp.pad(parts[node], ((0, 0), (i_bit, 1 - i_bit), (j_bit, 1 - j_bit), (l_bit, 1 - l_bit)))
        return total[:, :total_x, :total_y]

    def operate(field):
        images = jnp.einsum("xyzde,xyze->xyzd", stiffness, spread(field), precision=lax.Precision.HIGHEST)
        return collect(images) + tikhonov * field

    rhs = collect(loads)
    increment = jnp.zeros_like(rhs)
    cg_residual = rhs
    direction = rhs
    norm_now = jnp.sum(cg_residual * cg_residual)
    for sweep in range(ITERS):
        image = operate(direction)
        step_size = norm_now / jnp.sum(direction * image)
        increment = increment + step_size * direction
        cg_residual = cg_residual - step_size * image
        norm_next = jnp.sum(cg_residual * cg_residual)
        direction = cg_residual + (norm_next / norm_now) * direction
        norm_now = norm_next
    return increment, cg_residual
```

```python
import functools

import numpy as np

import jax
import jax.numpy as jnp
from jax import lax
from jax.experimental import pallas as pl
from jax.experimental.pallas import tpu as pltpu
from jax.sharding import PartitionSpec as P

F32 = jnp.float32
BF16 = jnp.bfloat16
TX, TY, TZ = 16, 32, 4
ROWS = TX * TY
COL = TZ * 512
PITCH = 40
GRID = 1024
HROWS = 112
TIKHONOV = 8.0
SCALE = 2.0**-8
PAIRS = [(0, 0), (0, 1), (0, 2), (1, 1), (1, 2), (2, 2)]
DOTS = [(0, 0), (0, 1), (0, 2), (0, 3), (1, 1), (1, 2), (1, 3), (2, 2), (2, 3)]
VMEM_LIMIT = 56 * 1024 * 1024


def voxel_factors():
    v = np.arange(512)
    coords = [(v // 64 + 0.5) / 8.0, (v // 8 % 8 + 0.5) / 8.0, (v % 8 + 0.5) / 8.0]
    return [(1.0 - t, t) for t in coords]


def hessian_table():
    s = voxel_factors()
    q = [(a * a, a * b, b * b) for a, b in s]
    table = np.zeros((HROWS, TZ, 512))
    for tj in range(3):
        for tl in range(3):
            for ti in range(3):
                t = (tj * 3 + tl) * 3 + ti
                for ez in range(TZ):
                    table[4 * t + ez, ez] = q[0][ti] * q[1][tj] * q[2][tl]
    return table.reshape(HROWS, COL).astype(jnp.bfloat16)


def load_table():
    s = voxel_factors()
    table = np.zeros((32, TZ, 512), np.float32)
    for j in range(2):
        for l in range(2):
            for i in range(2):
                for ez in range(TZ):
                    table[(j * 2 + l) * 8 + i * 4 + ez, ez] = s[0][i] * s[1][j] * s[2][l]
    table = table.reshape(32, COL)
    high = table.astype(jnp.bfloat16)
    low = (table - high.astype(np.float32)).astype(jnp.bfloat16)
    return np.concatenate([high, low], axis=0)


def edge_maps(low, high, xlo_lanes, xhi_lanes):
    ysend, ycoord = [], []
    for x in range(TX):
        for k in range(low):
            ysend.append(x * TY + TY - low + k)
            ycoord.append((x, k - low))
    for x in range(TX):
        for k in range(high):
            ysend.append(x * TY + k)
            ycoord.append((x, TY + k))
    lane_of = {c: n for n, c in enumerate(ycoord)}

    def strip(first, count, base):
        lanes, coord = [], []
        for x in range(first, first + count):
            for y in range(TY):
                lanes.append(x * TY + y)
                coord.append((x + base, y))
        for ys in (range(-low, 0), range(TY, TY + high)):
            for x in range(first, first + count):
                for y in ys:
                    lanes.append(ROWS + lane_of[(x, y)])
                    coord.append((x + base, y))
        return lanes, coord

    up, up_coord = strip(TX - low, low, -TX)
    down, down_coord = strip(0, high, TX)
    source = {}
    for x in range(TX):
        for y in range(TY):
            source[(x, y)] = x * TY + y
    for n, c in enumerate(ycoord):
        source[c] = ROWS + n
    for n, c in enumerate(up_coord):
        source[c] = ROWS + 128 + n
    for n, c in enumerate(down_coord):
        source[c] = ROWS + 128 + xlo_lanes + n
    grid = np.full((GRID,), -1)
    for (x, y), lane in source.items():
        grid[(x + 4) * PITCH + y + 4] = lane

    def row(values, lanes):
        out = np.full((1, lanes), -1, np.int32)
        out[0, : len(values)] = values
        return out

    xsend = np.concatenate([row(up, xlo_lanes), row(down, xhi_lanes)], axis=1)
    return row(ysend, 128), xsend, row(list(grid), GRID), low * TX


H_YSEND, H_XSEND, H_GRID, H_YLOW = edge_maps(3, 2, 128, 128)
L_YSEND, L_XSEND, L_GRID, L_YLOW = edge_maps(4, 3, 256, 128)
OWN_MAP = np.array(
    [[(x + 4) * PITCH + y + 4 for x in range(TX) for y in range(TY)]], np.int32
)


def onehot(index_row, depth):
    lanes = index_row.shape[1]
    rows = lax.broadcasted_iota(jnp.int32, (depth, lanes), 0)
    return jnp.where(rows == index_row, 1.0, 0.0).astype(BF16)


def select_lanes(value, choice, parts):
    total = None
    rest = value
    for part in range(parts):
        piece = rest.astype(BF16)
        term = jnp.dot(piece, choice, preferred_element_type=F32)
        total = term if total is None else total + term
        if part + 1 < parts:
            rest = rest - piece.astype(F32)
    return total


def matmul_nt(a, b):
    return lax.dot_general(a, b, (((1,), (1,)), ((), ())), preferred_element_type=F32)


def hessian_kernel(g_ref, m_ref, table_ref, index_ref, c_ref, cy_ref):
    step = pl.program_id(0)
    mask = m_ref[...].astype(F32).astype(BF16)
    for k, (c, d) in enumerate(PAIRS):
        x = (g_ref[c] * mask) * g_ref[d]
        c_ref[k * HROWS : (k + 1) * HROWS, :] = matmul_nt(table_ref[...], x)
    choice = onehot(index_ref[...] - step * 256, 256)
    part = select_lanes(c_ref[...], choice, 2)

    @pl.when(step == 0)
    def _():
        cy_ref[...] = part

    @pl.when(step > 0)
    def _():
        cy_ref[...] += part


def edge_kernel(ylow, own_ref, below_ref, above_ref, index_ref, y_ref, up_ref, down_ref):
    lane = lax.broadcasted_iota(jnp.int32, below_ref.shape, 1)
    ytile = jnp.where(lane < ylow, below_ref[...], above_ref[...])
    y_ref[...] = ytile
    source = jnp.concatenate([own_ref[...], ytile], axis=1)
    sent = select_lanes(source, onehot(index_ref[...], ROWS + 128), 2)
    ups = up_ref.shape[1]
    up_ref[...] = sent[:, :ups]
    down_ref[...] = sent[:, ups:]


def grid_kernel(own_ref, y_ref, xlo_ref, xhi_ref, index_ref, out_ref):
    source = jnp.concatenate([own_ref[...], y_ref[...], xlo_ref[...], xhi_ref[...]], axis=1)
    placed = select_lanes(source, onehot(index_ref[...], source.shape[1]), 2)
    for tile in range(GRID // 128):
        out_ref[tile] = placed[:, tile * 128 : (tile + 1) * 128]


def sample_slot(x, y):
    ymid = (y >= 0) & (y < TY)
    ylo = y < 0
    xmid = (x >= 0) & (x < TX)
    xlo = x < 0
    own = x * TY + y
    below = 512 + (x + 4) * TY + y
    above = 640 + (x - TX) * TY + y
    mid = jnp.where(xmid, own, jnp.where(xlo, below, above))
    left = jnp.where(
        xmid,
        800 + x * 4 + y + 4,
        jnp.where(xlo, 928 + (x + 4) * 4 + y + 4, 960 + (x - TX) * 4 + y + 4),
    )
    right = jnp.where(
        xmid,
        864 + x * 4 + y - TY,
        jnp.where(xlo, 944 + (x + 4) * 4 + y - TY, 992 + (x - TX) * 4 + y - TY),
    )
    return jnp.where(ymid, mid, jnp.where(ylo, left, right))


GHOST_AT = (0, 128, 288, 352, 416, 432, 448, 480)
GHOST_ROWS = (128, 160, 64, 64, 16, 16, 20, 20)


def warp_kernel(
    s_ref, w_ref, m_ref, g_ref, d_ref, p0, p1, p2, p3, p4, p5, p6, p7,
    o_ref, table_ref, index_ref, l_ref, ly_ref, ghost, image,
):
    ez = pl.program_id(0)
    ghost[448:512, :] = jnp.zeros((64, 512), BF16)
    for at, rows, piece in zip(GHOST_AT, GHOST_ROWS, (p0, p1, p2, p3, p4, p5, p6, p7)):
        ghost[at : at + rows, :] = piece[...]
    pick = lax.broadcasted_iota(jnp.int32, (ROWS, TZ), 1) == ez
    ox = jnp.sum(jnp.where(pick, o_ref[0], 0), axis=1, keepdims=True)
    oy = jnp.sum(jnp.where(pick, o_ref[1], 0), axis=1, keepdims=True)
    pos = lax.broadcasted_iota(jnp.int32, (ROWS, 1), 0)
    x = (pos >> 5) + ox
    y = (pos & 31) + oy
    near_slot = sample_slot(x, y)
    far_slot = sample_slot(x + 1, y)
    chunk = 256
    for first in range(0, ROWS, chunk):
        rows = slice(first, first + chunk)
        slot = jnp.concatenate([near_slot[rows], far_slot[rows]], axis=0)
        lane = lax.broadcasted_iota(jnp.int32, (2 * chunk, 512), 1)
        own = jnp.where(lane == slot, 1.0, 0.0).astype(BF16)
        other = jnp.where(lane + 512 == slot, 1.0, 0.0).astype(BF16)
        both = jnp.dot(own, d_ref[...], preferred_element_type=F32) + jnp.dot(
            other, ghost[...], preferred_element_type=F32
        )
        w = w_ref[rows, :].astype(F32)
        warped = w * both[:chunk] + (1.0 - w) * both[chunk:]
        resid = (s_ref[rows, :].astype(F32) - warped).astype(BF16)
        weighted = resid * m_ref[rows, :].astype(F32).astype(BF16)
        for c in range(3):
            image[c, rows, :] = g_ref[c, rows, :] * weighted

    @pl.when(ez == 0)
    def _():
        l_ref[...] = jnp.zeros_like(l_ref)

    for c in range(3):
        part = matmul_nt(table_ref[...], image[c])
        l_ref[c * 32 : (c + 1) * 32, :] += part[:32] + part[32:]

    @pl.when(ez == TZ - 1)
    def _():
        ly_ref[...] = select_lanes(l_ref[...], onehot(index_ref[...], ROWS), 2)


def powers_kernel(
    edge_ref, own_ref, y_ref, xlo_ref, xhi_ref, index_ref, coord_ref, own_index_ref, h_ref,
    v_ref, dots_ref, us, fs,
):
    row = lax.broadcasted_iota(jnp.int32, (8, GRID), 0)
    beyond_x = (coord_ref[0:1, :] >= TX) & (edge_ref[0] == 1)
    beyond_y = (coord_ref[1:2, :] >= TY) & (edge_ref[1] == 1)
    live = jnp.where(beyond_x | beyond_y, 0.0, 1.0)

    def scatter(f):
        out = []
        for c in range(3):
            sums = []
            for l in range(2):
                both = f(0, l, c) + pltpu.roll(f(1, l, c), 1, axis=1)
                split = jnp.where(row < 4, both, pltpu.roll(both, PITCH, axis=1))
                sums.append(split + pltpu.roll(split, 4, axis=0))
            a, b = sums
            lower = a + jnp.where((row & 3) == 0, 0.0, pltpu.roll(b, 1, axis=0))
            upper = b + jnp.where((row & 3) == 3, 0.0, pltpu.roll(a, 7, axis=0))
            out.append((lower * live, upper * live))
        return out

    def apply(u):
        for i in range(2):
            for j in range(2):
                shift = i * PITCH + j
                for d in range(3):
                    for l in range(2):
                        value = u[d][l]
                        if shift:
                            value = pltpu.roll(value, GRID - shift, axis=1)
                        us[((i * 2 + j) * 3 + d) * 2 + l] = value

        def tile_step(tile, carry):
            lanes = pl.ds(pl.multiple_of(tile * 128, 128), 128)
            uu = [us[k, :, lanes] for k in range(24)]
            acc = {}
            for k, (c, d) in enumerate(PAIRS):
                for tj in range(3):
                    for tl in range(3):
                        for i in range(2):
                            at = k * HROWS + (tj * 3 + tl) * 12 + i * 4
                            h = h_ref[tile, at : at + 8, :]
                            for mj in range(2):
                                nj = tj - mj
                                if nj not in (0, 1):
                                    continue
                                for ml in range(2):
                                    nl = tl - ml
                                    if nl not in (0, 1):
                                        continue
                                    for out_c, in_d in {(c, d), (d, c)}:
                                        term = h * uu[((i * 2 + mj) * 3 + in_d) * 2 + ml]
                                        key = (nj * 2 + nl) * 3 + out_c
                                        acc[key] = term if key not in acc else acc[key] + term
            for key in range(12):
                fs[key, :, lanes] = acc[key] * SCALE
            return carry

        lax.fori_loop(0, GRID // 128, tile_step, 0)
        return scatter(lambda j, l, c: fs[(j * 2 + l) * 3 + c])

    source = jnp.concatenate([own_ref[...], y_ref[...], xlo_ref[...], xhi_ref[...]], axis=1)
    loads = select_lanes(source, onehot(index_ref[...], source.shape[1]), 2)

    def load_rows(j, l, c):
        at = c * 32 + (j * 2 + l) * 8
        return loads[at : at + 8, :]

    vectors = [scatter(load_rows)]
    for _ in range(3):
        vectors.append(apply(vectors[-1]))
    pieces = []
    for vec in vectors:
        for lower, upper in vec:
            pieces.append(
                jnp.where(row < 4, lower, jnp.where(row == 4, pltpu.roll(upper, 1, axis=0), 0.0))
            )
    own = select_lanes(jnp.concatenate(pieces, axis=0), onehot(own_index_ref[...], GRID), 3)
    v_ref[...] = own
    lane = lax.broadcasted_iota(jnp.int32, (1, 128), 1)
    dots = jnp.zeros((1, 128), F32)
    for k, (a, b) in enumerate(DOTS):
        product = own[a * 24 : a * 24 + 24] * own[b * 24 : b * 24 + 24]
        total = jnp.sum(jnp.sum(product, axis=0, keepdims=True), axis=1, keepdims=True)
        dots = jnp.where(lane == k, total, dots)
    dots_ref[...] = jnp.broadcast_to(dots, dots_ref.shape)


def combine_kernel(v_ref, dots_ref, x_ref, r_ref):
    total = jnp.sum(dots_ref[...], axis=0, keepdims=True)
    gram = {}
    for k, (a, b) in enumerate(DOTS):
        gram[(a, b)] = gram[(b, a)] = total[:, k : k + 1]

    def inner(p, q):
        out = None
        for a, pa in p.items():
            for b, qb in q.items():
                term = pa * qb * gram[(a, b)]
                out = term if out is None else out + term
        return out

    def add(p, q, factor):
        out = dict(p)
        for a, qa in q.items():
            term = factor * qa
            out[a] = out[a] + term if a in out else term
        return out

    one = jnp.ones((1, 1), F32)
    increment, resid, direction = {}, {0: one}, {0: one}
    norm_now = gram[(0, 0)]
    for sweep in range(3):
        image = {}
        for a, pa in direction.items():
            image[a] = image[a] + TIKHONOV * pa if a in image else TIKHONOV * pa
            image[a + 1] = pa * (1.0 / SCALE)
        step_size = norm_now / inner(direction, image)
        increment = add(increment, direction, step_size)
        resid = add(resid, image, -step_size)
        if sweep < 2:
            norm_next = inner(resid, resid)
            direction = add(resid, direction, norm_next / norm_now)
            norm_now = norm_next
    for ref, coefs in ((x_ref, increment), (r_ref, resid)):
        for c in range(3):
            out = None
            for k, coef in coefs.items():
                at = (k * 3 + c) * 8
                term = coef * v_ref[at : at + 8, :]
                out = term if out is None else out + term
            ref[c] = jnp.transpose(out, (1, 0))[:, :5]


def whole(shape):
    return pl.BlockSpec(shape, lambda *_: (0,) * len(shape))


def call(kernel, outs, *args, name):
    return pl.pallas_call(
        kernel,
        out_shape=outs,
        in_specs=[pl.BlockSpec(memory_space=pltpu.VMEM)] * len(args),
        out_specs=jax.tree.map(lambda _: pl.BlockSpec(memory_space=pltpu.VMEM), outs),
        compiler_params=pltpu.CompilerParams(vmem_limit_bytes=VMEM_LIMIT),
        name=name,
    )(*args)


def struct(*shape):
    return jax.ShapeDtypeStruct(shape, F32)


def shifted(value, dx, dy):
    nx, ny = lax.axis_size("gx"), lax.axis_size("gy")
    pairs = []
    for x in range(nx):
        for y in range(ny):
            if 0 <= x + dx < nx and 0 <= y + dy < ny:
                pairs.append((x * ny + y, (x + dx) * ny + y + dy))
    return lax.ppermute(value, ("gx", "gy"), pairs)


def exchange(own, ysend, xsend, ylow, widths, name):
    rows = own.shape[0]
    below, above = shifted(ysend, 0, 1), shifted(ysend, 0, -1)
    ytile, up, down = call(
        functools.partial(edge_kernel, ylow),
        (struct(rows, 128), struct(rows, widths[0]), struct(rows, widths[1])),
        own, below, above, jnp.asarray(xsend),
        name=name,
    )
    return ytile, shifted(up, 1, 0), shifted(down, -1, 0)


def per_device(
    reference_scan, ref_gradient, deformed_scan, interp_weights, sample_mask, block_list, offsets
):
    scan = reference_scan.reshape(ROWS, COL)
    grad = ref_gradient.reshape(3, ROWS, COL)
    weights = interp_weights.reshape(ROWS, COL)
    mask = sample_mask.reshape(ROWS, COL)
    moved = deformed_scan.reshape(ROWS, COL)
    ylast = deformed_scan[:, TY - 4 :, :].reshape(TX * 4, COL)
    yfirst = deformed_scan[:, :4, :].reshape(TX * 4, COL)
    pieces = (
        shifted(moved[384:], 1, 0),
        shifted(moved[:160], -1, 0),
        shifted(ylast, 0, 1),
        shifted(yfirst, 0, -1),
        shifted(ylast[48:], 1, 1),
        shifted(yfirst[48:], 1, -1),
        shifted(ylast[:20], -1, 1),
        shifted(yfirst[:20], -1, -1),
    )
    coefs, coefs_y = pl.pallas_call(
        hessian_kernel,
        out_shape=(struct(6 * HROWS, ROWS), struct(6 * HROWS, 128)),
        grid=(2,),
        in_specs=[
            pl.BlockSpec((3, 256, COL), lambda i: (0, i, 0)),
            pl.BlockSpec((256, COL), lambda i: (i, 0)),
            whole((HROWS, COL)),
            whole((1, 128)),
        ],
        out_specs=(pl.BlockSpec((6 * HROWS, 256), lambda i: (0, i)), whole((6 * HROWS, 128))),
        compiler_params=pltpu.CompilerParams(vmem_limit_bytes=VMEM_LIMIT),
        name="hessian",
    )(grad, mask, jnp.asarray(hessian_table()), jnp.asarray(H_YSEND))
    coefs_ghost = exchange(coefs, coefs_y, H_XSEND, H_YLOW, (128, 128), "hessian_edges")

    lanes = lambda rows: pl.BlockSpec((rows, 512), lambda i: (0, i))
    loads, loads_y = pl.pallas_call(
        warp_kernel,
        out_shape=(struct(96, ROWS), struct(96, 128)),
        grid=(TZ,),
        in_specs=[
            lanes(ROWS), lanes(ROWS), lanes(ROWS),
            pl.BlockSpec((3, ROWS, 512), lambda i: (0, 0, i)),
            lanes(ROWS),
            *[lanes(rows) for rows in GHOST_ROWS],
            whole((2, ROWS, TZ)),
            lanes(64),
            whole((1, 128)),
        ],
        out_specs=(whole((96, ROWS)), whole((96, 128))),
        scratch_shapes=[pltpu.VMEM((512, 512), BF16), pltpu.VMEM((3, ROWS, 512), BF16)],
        compiler_params=pltpu.CompilerParams(vmem_limit_bytes=VMEM_LIMIT),
        name="warp",
    )(
        scan, weights, mask, grad, moved, *pieces, offsets.reshape(2, ROWS, TZ),
        jnp.asarray(load_table()), jnp.asarray(L_YSEND),
    )
    loads_ghost = exchange(loads, loads_y, L_XSEND, L_YLOW, (256, 128), "load_edges")
    stiffness = call(
        grid_kernel, struct(GRID // 128, 6 * HROWS, 128), coefs, *coefs_ghost,
        jnp.asarray(H_GRID), name="hessian_grid",
    )

    position = np.arange(GRID)
    coord = np.stack([position // PITCH - 4, position % PITCH - 4]).astype(np.int32)
    last = jnp.stack(
        [lax.axis_index("gx") == lax.axis_size("gx") - 1, lax.axis_index("gy") == lax.axis_size("gy") - 1]
    ).astype(jnp.int32)
    vmem = pl.BlockSpec(memory_space=pltpu.VMEM)
    devices = lax.axis_size("gx") * lax.axis_size("gy")
    vectors, dots = pl.pallas_call(
        powers_kernel,
        out_shape=(struct(96, ROWS), struct(devices, 128)),
        in_specs=[pl.BlockSpec(memory_space=pltpu.SMEM)] + [vmem] * 8,
        out_specs=(vmem, vmem),
        scratch_shapes=[pltpu.VMEM((24, 8, GRID), F32), pltpu.VMEM((12, 8, GRID), F32)],
        compiler_params=pltpu.CompilerParams(vmem_limit_bytes=VMEM_LIMIT),
        name="powers",
    )(
        last, loads, *loads_ghost, jnp.asarray(L_GRID), jnp.asarray(coord),
        jnp.asarray(OWN_MAP), stiffness,
    )
    dots = lax.all_to_all(dots, ("gx", "gy"), 0, 0, tiled=True)
    increment, resid = call(
        combine_kernel, (struct(3, ROWS, 5), struct(3, ROWS, 5)), vectors, dots, name="combine"
    )
    return (increment.reshape(3, TX, TY, 5), resid.reshape(3, TX, TY, 5))


def solution(mesh):
    return jax.shard_map(
        per_device,
        mesh=mesh,
        in_specs=(
            P("gx", "gy", None),
            P(None, "gx", "gy", None),
            P("gx", "gy", None),
            P("gx", "gy", None),
            P("gx", "gy", None),
            P("gx", "gy"),
            P(None, "gx", "gy", None),
        ),
        out_specs=(P(None, "gx", "gy", None), P(None, "gx", "gy", None)),
        check_vma=False,
    )
```

```python
import functools

import numpy as np

import jax
import jax.numpy as jnp
from jax import lax
from jax.experimental import pallas as pl
from jax.experimental.pallas import tpu as pltpu
from jax.sharding import PartitionSpec as P

F32 = jnp.float32
BF16 = jnp.bfloat16
TX, TY, TZ = 16, 32, 4
ROWS = TX * TY
COL = TZ * 512
PITCH = 40
GRID = 1024
HROWS = 112
CROWS = 6 * HROWS
TIKHONOV = 8.0
SCALE = 2.0**-8
PAIRS = [(0, 0), (0, 1), (0, 2), (1, 1), (1, 2), (2, 2)]
DOTS = [(0, 0), (0, 1), (0, 2), (0, 3), (1, 1), (1, 2), (1, 3), (2, 2), (2, 3)]
VMEM_LIMIT = 24 * 1024 * 1024


def voxel_factors():
    v = np.arange(512)
    coords = [(v // 64 + 0.5) / 8.0, (v // 8 % 8 + 0.5) / 8.0, (v % 8 + 0.5) / 8.0]
    return [(1.0 - t, t) for t in coords]


def hessian_table():
    s = voxel_factors()
    q = [(a * a, a * b, b * b) for a, b in s]
    table = np.zeros((HROWS, TZ, 512))
    for tj in range(3):
        for tl in range(3):
            for ti in range(3):
                t = (tj * 3 + tl) * 3 + ti
                for ez in range(TZ):
                    table[4 * t + ez, ez] = q[0][ti] * q[1][tj] * q[2][tl]
    return table.reshape(HROWS, COL).astype(jnp.bfloat16)


def load_table():
    s = voxel_factors()
    table = np.zeros((32, TZ, 512), np.float32)
    for j in range(2):
        for l in range(2):
            for i in range(2):
                for ez in range(TZ):
                    table[(j * 2 + l) * 8 + i * 4 + ez, ez] = s[0][i] * s[1][j] * s[2][l]
    table = table.reshape(32, COL)
    high = table.astype(jnp.bfloat16)
    low = (table - high.astype(np.float32)).astype(jnp.bfloat16)
    return np.concatenate([high, low], axis=0)


def edge_maps(low, high, xlo_lanes, xhi_lanes):
    ysend, ycoord = [], []
    for x in range(TX):
        for k in range(low):
            ysend.append(x * TY + TY - low + k)
            ycoord.append((x, k - low))
    for x in range(TX):
        for k in range(high):
            ysend.append(x * TY + k)
            ycoord.append((x, TY + k))
    lane_of = {c: n for n, c in enumerate(ycoord)}

    def strip(first, count, base):
        lanes, coord = [], []
        for x in range(first, first + count):
            for y in range(TY):
                lanes.append(x * TY + y)
                coord.append((x + base, y))
        for ys in (range(-low, 0), range(TY, TY + high)):
            for x in range(first, first + count):
                for y in ys:
                    lanes.append(ROWS + lane_of[(x, y)])
                    coord.append((x + base, y))
        return lanes, coord

    up, up_coord = strip(TX - low, low, -TX)
    down, down_coord = strip(0, high, TX)
    source = {}
    for x in range(TX):
        for y in range(TY):
            source[(x, y)] = x * TY + y
    for n, c in enumerate(ycoord):
        source[c] = ROWS + n
    for n, c in enumerate(up_coord):
        source[c] = ROWS + 128 + n
    for n, c in enumerate(down_coord):
        source[c] = ROWS + 128 + xlo_lanes + n
    grid = np.full((GRID,), -1)
    for (x, y), lane in source.items():
        grid[(x + 4) * PITCH + y + 4] = lane

    def row(values, lanes):
        out = np.full((1, lanes), -1, np.int32)
        out[0, : len(values)] = values
        return out

    xsend = np.concatenate([row(up, xlo_lanes), row(down, xhi_lanes)], axis=1)
    return row(ysend, 128), xsend, row(list(grid), GRID), low * TX


H_YSEND, H_XSEND, H_GRID, H_YLOW = edge_maps(3, 2, 128, 128)
L_YSEND, L_XSEND, L_GRID, L_YLOW = edge_maps(4, 3, 256, 128)
OWN_MAP = np.array(
    [[(x + 4) * PITCH + y + 4 for x in range(TX) for y in range(TY)]], np.int32
)


def onehot(index_row, depth):
    lanes = index_row.shape[1]
    rows = lax.broadcasted_iota(jnp.int32, (depth, lanes), 0)
    return jnp.where(rows == index_row, 1.0, 0.0).astype(BF16)


def select_lanes(value, choice, parts):
    total = None
    rest = value
    for part in range(parts):
        piece = rest.astype(BF16)
        term = jnp.dot(piece, choice, preferred_element_type=F32)
        total = term if total is None else total + term
        if part + 1 < parts:
            rest = rest - piece.astype(F32)
    return total


def matmul_nt(a, b):
    return lax.dot_general(a, b, (((1,), (1,)), ((), ())), preferred_element_type=F32)


def pack_y_kernel(end_ref, start_ref, last_ref, first_ref):
    row = lax.broadcasted_iota(jnp.int32, (64, 128), 0)
    pos = lax.broadcasted_iota(jnp.int32, (64, 128), 1)
    for ref, out_ref, at in ((end_ref, last_ref, 4), (start_ref, first_ref, 0)):
        choice = jnp.where(pos == (row >> 2) * 8 + (row & 3) + at, 1.0, 0.0).astype(BF16)
        rows = ref[...].astype(F32).reshape(TX * 8, ref.shape[-1]).astype(BF16)
        out_ref[...] = jnp.dot(choice, rows, preferred_element_type=F32).astype(BF16)


def pack_x_kernel(d_ref, ylo_ref, yhi_ref, up_ref, down_ref, sems):
    copies = []
    for source, start, rows, target, at in (
        (d_ref, 384, 128, up_ref, 0),
        (ylo_ref, 48, 16, up_ref, 128),
        (yhi_ref, 48, 16, up_ref, 144),
        (d_ref, 0, 160, down_ref, 0),
        (ylo_ref, 0, 24, down_ref, 160),
        (yhi_ref, 0, 24, down_ref, 184),
    ):
        copies.append(
            pltpu.make_async_copy(
                source.at[pl.ds(start, rows)], target.at[pl.ds(at, rows)], sems.at[len(copies)]
            )
        )
    for copy in copies:
        copy.start()
    for copy in copies:
        copy.wait()


def hessian_kernel(g_ref, m_ref, table_ref, yindex_ref, xindex_ref, c_ref, cy_ref, cx_ref):
    step = pl.program_id(0)
    mask = m_ref[...].astype(F32).astype(BF16)
    for k, (c, d) in enumerate(PAIRS):
        x = (g_ref[c] * mask) * g_ref[d]
        c_ref[k * HROWS : (k + 1) * HROWS, :] = matmul_nt(table_ref[...], x).astype(BF16)
    for index_ref, ref in ((yindex_ref, cy_ref), (xindex_ref, cx_ref)):
        choice = onehot(index_ref[...] - step * 256, 256)
        part = jnp.dot(c_ref[...], choice, preferred_element_type=F32).astype(BF16)

        @pl.when(step == 0)
        def _():
            ref[...] = part

        @pl.when(step > 0)
        def _():
            ref[...] += part


def edge_kernel(
    l_ref, cx_ref, below_ref, above_ref, cindex_ref, lindex_ref, y_ref, up_ref, down_ref
):
    lane = lax.broadcasted_iota(jnp.int32, (1, 128), 1)
    ytile_c = jnp.where(lane < H_YLOW, below_ref[:CROWS, :], above_ref[:CROWS, :])
    ytile_l = jnp.where(lane < L_YLOW, below_ref[CROWS:, :], above_ref[CROWS:, :])
    y_ref[:CROWS, :] = ytile_c
    y_ref[CROWS:, :] = ytile_l
    sent = jnp.dot(ytile_c, onehot(cindex_ref[...] - ROWS, 128), preferred_element_type=F32)
    sent = sent.astype(BF16) + cx_ref[...]
    up_ref[:CROWS, :] = sent[:, :128]
    down_ref[:CROWS, :] = sent[:, 128:]
    high = l_ref[...].astype(BF16)
    low = (l_ref[...] - high.astype(F32)).astype(BF16)
    source = jnp.concatenate([jnp.concatenate([high, low], axis=0), ytile_l], axis=1)
    sent = jnp.dot(
        source, onehot(lindex_ref[...], ROWS + 128), preferred_element_type=F32
    ).astype(BF16)
    up_ref[CROWS : CROWS + 192, :] = sent[:, :128]
    up_ref[CROWS + 192 :, :] = sent[:, 128:256]
    down_ref[CROWS:, :] = sent[:, 256:]


def grid_kernel(own_ref, index_ref, out_ref):
    placed = jnp.dot(own_ref[...], onehot(index_ref[...], ROWS), preferred_element_type=F32)
    for tile in range(GRID // 128):
        out_ref[tile] = placed[:, tile * 128 : (tile + 1) * 128]


def sample_slot(x, y):
    ymid = (y >= 0) & (y < TY)
    ylo = y < 0
    xmid = (x >= 0) & (x < TX)
    xlo = x < 0
    mid = jnp.where(
        xmid, x * TY + y, jnp.where(xlo, 512 + (x + 4) * TY + y, 672 + (x - TX) * TY + y)
    )
    left = jnp.where(xmid, 880 + x * 4, jnp.where(xlo, 640 + (x + 4) * 4, 832 + (x - TX) * 4))
    right = jnp.where(xmid, 944 + x * 4, jnp.where(xlo, 656 + (x + 4) * 4, 856 + (x - TX) * 4))
    return jnp.where(ymid, mid, jnp.where(ylo, left + y + 4, right + y - TY))


def slot_columns(o_ref, ez):
    layer = lax.broadcasted_iota(jnp.int32, (TX, TZ, TY), 1) == ez
    ox, oy = (jnp.sum(jnp.where(layer, o_ref[axis], 0), axis=1) for axis in range(2))
    x = lax.broadcasted_iota(jnp.int32, (TX, TY), 0) + ox
    y = lax.broadcasted_iota(jnp.int32, (TX, TY), 1) + oy
    near, far = sample_slot(x, y), sample_slot(x + 1, y)
    parts = jnp.concatenate([near >> 7, near & 127, far >> 7, far & 127], axis=1)
    row = lax.broadcasted_iota(jnp.int32, (ROWS, TX), 0)
    col = lax.broadcasted_iota(jnp.int32, (ROWS, TX), 1)
    spread = jnp.dot(
        jnp.where(row >> 5 == col, 1.0, 0.0).astype(BF16),
        parts.astype(F32).astype(BF16),
        preferred_element_type=F32,
    )
    row = lax.broadcasted_iota(jnp.int32, (ROWS, 128), 0)
    col = lax.broadcasted_iota(jnp.int32, (ROWS, 128), 1)
    spread = jnp.where(row & 31 == col & 31, spread, 0.0).astype(BF16)
    row = lax.broadcasted_iota(jnp.int32, (128, 512), 0)
    col = lax.broadcasted_iota(jnp.int32, (128, 512), 1)
    ones = jnp.where(row >> 5 == col >> 7, 1.0, 0.0).astype(BF16)
    out = jnp.dot(spread, ones, preferred_element_type=F32).astype(BF16)
    high = jnp.concatenate([out[:, :128], out[:, 256:384]], axis=0)
    low = jnp.concatenate([out[:, 128:256], out[:, 384:]], axis=0)
    return high, low


def slot_onehot(high, low, first):
    lane = lax.broadcasted_iota(jnp.int32, low.shape, 1).astype(F32).astype(BF16)
    zero = jnp.zeros(low.shape, BF16)
    hit = jnp.where(low == lane, jnp.ones(low.shape, BF16), zero)
    return jnp.concatenate([jnp.where(high == float(first + k), hit, zero) for k in range(4)], axis=1)


GHOST_AT = (0, 160, 368, 432)
GHOST_ROWS = (160, 208, 64, 64)


def own_samples_kernel(d_ref, o_ref, out_ref):
    ez = pl.program_id(0)
    high, low = slot_columns(o_ref, ez)
    out_ref[...] = jnp.dot(
        slot_onehot(high, low, 0), d_ref[...], preferred_element_type=F32
    ).astype(BF16)


def warp_kernel(
    s_ref, w_ref, m_ref, g_ref, n_ref, p0, p1, p2, p3, o_ref, table_ref, index_ref, cy_ref,
    l_ref, msg_ref, ghost, image,
):
    ez = pl.program_id(0)
    ghost[496:512, :] = jnp.zeros((16, 512), BF16)
    for at, rows, piece in zip(GHOST_AT, GHOST_ROWS, (p0, p1, p2, p3)):
        ghost[at : at + rows, :] = piece[...]
    high, low = slot_columns(o_ref, ez)
    both = jnp.dot(
        slot_onehot(high, low, 4), ghost[...], preferred_element_type=F32
    ) + n_ref[...].astype(F32)
    w = w_ref[...].astype(F32)
    warped = w * both[:ROWS] + (1.0 - w) * both[ROWS:]
    resid = (s_ref[...].astype(F32) - warped).astype(BF16)
    weighted = resid * m_ref[...].astype(F32).astype(BF16)
    for c in range(3):
        image[c] = g_ref[c] * weighted

    @pl.when(ez == 0)
    def _():
        l_ref[...] = jnp.zeros_like(l_ref)

    for c in range(3):
        part = matmul_nt(table_ref[...], image[c])
        l_ref[c * 32 : (c + 1) * 32, :] += part[:32] + part[32:]

    @pl.when(ez == TZ - 1)
    def _():
        choice = onehot(index_ref[...], ROWS)
        loads = l_ref[...]
        top = loads.astype(BF16)
        rest = (loads - top.astype(F32)).astype(BF16)
        msg_ref[:CROWS, :] = cy_ref[...]
        msg_ref[CROWS:, :] = jnp.dot(
            jnp.concatenate([top, rest], axis=0), choice, preferred_element_type=F32
        ).astype(BF16)


def powers_kernel(
    edge_ref, own_ref, y_ref, xlo_ref, xhi_ref, cindex_ref, index_ref, coord_ref, own_index_ref,
    hown_ref, v_ref, dots_ref, us, fs, h_ref,
):
    row = lax.broadcasted_iota(jnp.int32, (8, GRID), 0)
    beyond_x = (coord_ref[0:1, :] >= TX) & (edge_ref[0] == 1)
    beyond_y = (coord_ref[1:2, :] >= TY) & (edge_ref[1] == 1)
    live = jnp.where(beyond_x | beyond_y, 0.0, 1.0)

    def scatter(f):
        out = []
        for c in range(3):
            sums = []
            for l in range(2):
                both = f(0, l, c) + pltpu.roll(f(1, l, c), 1, axis=1)
                split = jnp.where(row < 4, both, pltpu.roll(both, PITCH, axis=1))
                sums.append(split + pltpu.roll(split, 4, axis=0))
            a, b = sums
            lower = a + jnp.where((row & 3) == 0, 0.0, pltpu.roll(b, 1, axis=0))
            upper = b + jnp.where((row & 3) == 3, 0.0, pltpu.roll(a, 7, axis=0))
            out.append((lower * live, upper * live))
        return out

    def apply(u):
        for i in range(2):
            for j in range(2):
                shift = i * PITCH + j
                for d in range(3):
                    for l in range(2):
                        value = u[d][l]
                        if shift:
                            value = pltpu.roll(value, GRID - shift, axis=1)
                        us[((i * 2 + j) * 3 + d) * 2 + l] = value

        def tile_step(tile, carry):
            lanes = pl.ds(pl.multiple_of(tile * 128, 128), 128)
            uu = [us[k, :, lanes] for k in range(24)]
            acc = {}
            for k, (c, d) in enumerate(PAIRS):
                for tj in range(3):
                    for tl in range(3):
                        for i in range(2):
                            at = k * HROWS + (tj * 3 + tl) * 12 + i * 4
                            h = h_ref[tile, at : at + 8, :]
                            for mj in range(2):
                                nj = tj - mj
                                if nj not in (0, 1):
                                    continue
                                for ml in range(2):
                                    nl = tl - ml
                                    if nl not in (0, 1):
                                        continue
                                    for out_c, in_d in {(c, d), (d, c)}:
                                        term = h * uu[((i * 2 + mj) * 3 + in_d) * 2 + ml]
                                        key = (nj * 2 + nl) * 3 + out_c
                                        acc[key] = term if key not in acc else acc[key] + term
            for key in range(12):
                fs[key, :, lanes] = acc[key] * SCALE
            return carry

        lax.fori_loop(0, GRID // 128, tile_step, 0)
        return scatter(lambda j, l, c: fs[(j * 2 + l) * 3 + c])

    ghosts = jnp.concatenate([y_ref[:CROWS, :], xlo_ref[:CROWS, :], xhi_ref[:CROWS, :]], axis=1)
    placed = jnp.dot(ghosts, onehot(cindex_ref[...] - ROWS, 384), preferred_element_type=F32)
    for tile in range(GRID // 128):
        h_ref[tile] = placed[:, tile * 128 : (tile + 1) * 128] + hown_ref[tile]
    top = own_ref[...].astype(BF16)
    rest = (own_ref[...] - top.astype(F32)).astype(BF16)
    source = jnp.concatenate(
        [
            jnp.concatenate([top, rest], axis=0),
            y_ref[CROWS:, :],
            xlo_ref[CROWS : CROWS + 192, :],
            xlo_ref[CROWS + 192 :, :],
            xhi_ref[CROWS:, :],
        ],
        axis=1,
    )
    loads = jnp.dot(source, onehot(index_ref[...], GRID), preferred_element_type=F32)
    loads = loads[:96] + loads[96:]

    def load_rows(j, l, c):
        at = c * 32 + (j * 2 + l) * 8
        return loads[at : at + 8, :]

    vectors = [scatter(load_rows)]
    for _ in range(3):
        vectors.append(apply(vectors[-1]))
    pieces = []
    for vec in vectors:
        for lower, upper in vec:
            pieces.append(
                jnp.where(row < 4, lower, jnp.where(row == 4, pltpu.roll(upper, 1, axis=0), 0.0))
            )
    own = select_lanes(jnp.concatenate(pieces, axis=0), onehot(own_index_ref[...], GRID), 3)
    v_ref[...] = own
    lane = lax.broadcasted_iota(jnp.int32, (1, 128), 1)
    dots = jnp.zeros((1, 128), F32)
    for k, (a, b) in enumerate(DOTS):
        product = own[a * 24 : a * 24 + 24] * own[b * 24 : b * 24 + 24]
        total = jnp.sum(jnp.sum(product, axis=0, keepdims=True), axis=1, keepdims=True)
        dots = jnp.where(lane == k, total, dots)
    dots_ref[...] = jnp.broadcast_to(dots, dots_ref.shape)


def combine_kernel(v_ref, dots_ref, x_ref, r_ref):
    total = jnp.sum(dots_ref[...], axis=0, keepdims=True)
    gram = {}
    for k, (a, b) in enumerate(DOTS):
        gram[(a, b)] = gram[(b, a)] = total[:, k : k + 1]

    def inner(p, q):
        out = None
        for a, pa in p.items():
            for b, qb in q.items():
                term = pa * qb * gram[(a, b)]
                out = term if out is None else out + term
        return out

    def add(p, q, factor):
        out = dict(p)
        for a, qa in q.items():
            term = factor * qa
            out[a] = out[a] + term if a in out else term
        return out

    one = jnp.ones((1, 1), F32)
    increment, resid, direction = {}, {0: one}, {0: one}
    norm_now = gram[(0, 0)]
    for sweep in range(3):
        image = {}
        for a, pa in direction.items():
            image[a] = image[a] + TIKHONOV * pa if a in image else TIKHONOV * pa
            image[a + 1] = pa * (1.0 / SCALE)
        step_size = norm_now / inner(direction, image)
        increment = add(increment, direction, step_size)
        resid = add(resid, image, -step_size)
        if sweep < 2:
            norm_next = inner(resid, resid)
            direction = add(resid, direction, norm_next / norm_now)
            norm_now = norm_next
    at_x = lax.broadcasted_iota(jnp.int32, (TX, ROWS), 1) >> 5 == lax.broadcasted_iota(
        jnp.int32, (TX, ROWS), 0
    )
    at_y = lax.broadcasted_iota(jnp.int32, (ROWS, TY), 0) & 31 == lax.broadcasted_iota(
        jnp.int32, (ROWS, TY), 1
    )
    pieces = []
    for coefs in (increment, resid):
        for c in range(3):
            out = None
            for k, coef in coefs.items():
                at = (k * 3 + c) * 8
                term = coef * v_ref[at : at + 8, :]
                out = term if out is None else out + term
            for z in range(TZ + 1):
                pieces.append(jnp.where(at_x, out[z : z + 1, :], 0.0))
    split = select_lanes(
        jnp.concatenate(pieces, axis=0), jnp.where(at_y, 1.0, 0.0).astype(BF16), 3
    )
    half = 3 * (TZ + 1) * TX
    x_ref[...] = split[:half]
    r_ref[...] = split[half:]


def whole(shape):
    return pl.BlockSpec(shape, lambda *_: (0,) * len(shape))


def call(kernel, outs, *args, name, us):
    return pl.pallas_call(
        kernel,
        out_shape=outs,
        in_specs=[pl.BlockSpec(memory_space=pltpu.VMEM)] * len(args),
        out_specs=jax.tree.map(lambda _: pl.BlockSpec(memory_space=pltpu.VMEM), outs),
        compiler_params=pltpu.CompilerParams(vmem_limit_bytes=VMEM_LIMIT),
        cost_estimate=cost(us),
        name=name,
    )(*args)


def struct(*shape, dtype=F32):
    return jax.ShapeDtypeStruct(shape, dtype)


def cost(us):
    return pl.CostEstimate(flops=0, transcendentals=0, bytes_accessed=int(us * 3.0e6))


def shifted(value, dx, dy):
    nx, ny = lax.axis_size("gx"), lax.axis_size("gy")
    pairs = []
    for x in range(nx):
        for y in range(ny):
            if 0 <= x + dx < nx and 0 <= y + dy < ny:
                pairs.append((x * ny + y, (x + dx) * ny + y + dy))
    return lax.ppermute(value, ("gx", "gy"), pairs)


def per_device(
    reference_scan, ref_gradient, deformed_scan, interp_weights, sample_mask, block_list, offsets
):
    scan = reference_scan.reshape(ROWS, COL)
    grad = ref_gradient.reshape(3, ROWS, COL)
    weights = interp_weights.reshape(ROWS, COL)
    mask = sample_mask.reshape(ROWS, COL)
    moved = deformed_scan.reshape(ROWS, COL)
    moves = jnp.transpose(offsets, (0, 1, 3, 2))
    lanes = lambda rows: pl.BlockSpec((rows, 512), lambda i: (0, i))
    params = pltpu.CompilerParams(vmem_limit_bytes=VMEM_LIMIT)
    bf = functools.partial(struct, dtype=BF16)

    ends = deformed_scan.reshape(TX, TY // 8, 8, COL)
    ylast, yfirst = pl.pallas_call(
        pack_y_kernel,
        out_shape=(bf(64, COL), bf(64, COL)),
        grid=(2,),
        in_specs=[
            pl.BlockSpec((TX, None, 8, COL // 2), lambda i: (0, TY // 8 - 1, 0, i)),
            pl.BlockSpec((TX, None, 8, COL // 2), lambda i: (0, 0, 0, i)),
        ],
        out_specs=(pl.BlockSpec((64, COL // 2), lambda i: (0, i)),) * 2,
        compiler_params=params,
        cost_estimate=cost(2),
        name="pack_y",
    )(ends, ends)
    ylo, yhi = shifted(ylast, 0, 1), shifted(yfirst, 0, -1)
    anywhere = pl.BlockSpec(memory_space=pl.ANY)
    up, down = pl.pallas_call(
        pack_x_kernel,
        out_shape=(bf(160, COL), bf(208, COL)),
        in_specs=[anywhere] * 3,
        out_specs=(anywhere, anywhere),
        scratch_shapes=[pltpu.SemaphoreType.DMA((6,))],
        compiler_params=params,
        cost_estimate=cost(2),
        name="pack_x",
    )(moved, ylo, yhi)
    grad, mask, moves, up, down = lax.optimization_barrier((grad, mask, moves, up, down))
    xlo, xhi = shifted(up, 1, 0), shifted(down, -1, 0)

    coefs, coefs_y, coefs_x = pl.pallas_call(
        hessian_kernel,
        out_shape=(bf(CROWS, ROWS), bf(CROWS, 128), bf(CROWS, 256)),
        grid=(2,),
        in_specs=[
            pl.BlockSpec((3, 256, COL), lambda i: (0, i, 0)),
            pl.BlockSpec((256, COL), lambda i: (i, 0)),
            whole((HROWS, COL)),
            whole((1, 128)),
            whole((1, 256)),
        ],
        out_specs=(
            pl.BlockSpec((CROWS, 256), lambda i: (0, i)),
            whole((CROWS, 128)),
            whole((CROWS, 256)),
        ),
        compiler_params=params,
        cost_estimate=cost(9),
        name="hessian",
    )(
        grad, mask, jnp.asarray(hessian_table()), jnp.asarray(H_YSEND),
        jnp.asarray(np.where(H_XSEND < ROWS, H_XSEND, -1)),
    )
    own_samples = pl.pallas_call(
        own_samples_kernel,
        out_shape=bf(2 * ROWS, COL),
        grid=(TZ,),
        in_specs=[lanes(ROWS), whole((2, TX, TZ, TY))],
        out_specs=lanes(2 * ROWS),
        compiler_params=params,
        cost_estimate=cost(7),
        name="own_samples",
    )(moved, moves)
    stiffness = call(
        grid_kernel, struct(GRID // 128, CROWS, 128), coefs, jnp.asarray(H_GRID),
        name="hessian_grid", us=3,
    )

    loads, message = pl.pallas_call(
        warp_kernel,
        out_shape=(struct(96, ROWS), bf(CROWS + 192, 128)),
        grid=(TZ,),
        in_specs=[
            lanes(ROWS), lanes(ROWS), lanes(ROWS),
            pl.BlockSpec((3, ROWS, 512), lambda i: (0, 0, i)),
            lanes(2 * ROWS),
            *[lanes(rows) for rows in GHOST_ROWS],
            whole((2, TX, TZ, TY)),
            lanes(64),
            whole((1, 128)),
            whole((CROWS, 128)),
        ],
        out_specs=(whole((96, ROWS)), whole((CROWS + 192, 128))),
        scratch_shapes=[pltpu.VMEM((512, 512), BF16), pltpu.VMEM((3, ROWS, 512), BF16)],
        compiler_params=params,
        cost_estimate=cost(9),
        name="warp",
    )(
        scan, weights, mask, grad, own_samples, xlo, xhi, ylo, yhi, moves,
        jnp.asarray(load_table()), jnp.asarray(L_YSEND), coefs_y,
    )
    below, above = shifted(message, 0, 1), shifted(message, 0, -1)
    ytile, up, down = call(
        edge_kernel,
        (bf(CROWS + 192, 128), bf(CROWS + 384, 128), bf(CROWS + 192, 128)),
        loads, coefs_x, below, above, jnp.asarray(H_XSEND), jnp.asarray(L_XSEND),
        name="edges", us=2,
    )
    ghosts = (ytile, shifted(up, 1, 0), shifted(down, -1, 0))

    position = np.arange(GRID)
    coord = np.stack([position // PITCH - 4, position % PITCH - 4]).astype(np.int32)
    last = jnp.stack(
        [lax.axis_index("gx") == lax.axis_size("gx") - 1, lax.axis_index("gy") == lax.axis_size("gy") - 1]
    ).astype(jnp.int32)
    vmem = pl.BlockSpec(memory_space=pltpu.VMEM)
    devices = lax.axis_size("gx") * lax.axis_size("gy")
    vectors, dots = pl.pallas_call(
        powers_kernel,
        out_shape=(struct(96, ROWS), struct(devices, 128)),
        in_specs=[pl.BlockSpec(memory_space=pltpu.SMEM)] + [vmem] * 9,
        out_specs=(vmem, vmem),
        scratch_shapes=[
            pltpu.VMEM((24, 8, GRID), F32),
            pltpu.VMEM((12, 8, GRID), F32),
            pltpu.VMEM((GRID // 128, CROWS, 128), F32),
        ],
        compiler_params=params,
        cost_estimate=cost(9),
        name="powers",
    )(
        last, loads, *ghosts, jnp.asarray(H_GRID), jnp.asarray(L_GRID), jnp.asarray(coord),
        jnp.asarray(OWN_MAP), stiffness,
    )
    dots = lax.all_to_all(dots, ("gx", "gy"), 0, 0, tiled=True)
    increment, resid = call(
        combine_kernel, (struct(240, TY), struct(240, TY)), vectors, dots, name="combine", us=3
    )
    return tuple(
        jnp.transpose(out.reshape(3, TZ + 1, TX, TY), (0, 2, 3, 1)) for out in (increment, resid)
    )


def solution(mesh):
    return jax.shard_map(
        per_device,
        mesh=mesh,
        in_specs=(
            P("gx", "gy", None),
            P(None, "gx", "gy", None),
            P("gx", "gy", None),
            P("gx", "gy", None),
            P("gx", "gy", None),
            P("gx", "gy"),
            P(None, "gx", "gy", None),
        ),
        out_specs=(P(None, "gx", "gy", None), P(None, "gx", "gy", None)),
        check_vma=False,
    )
```

```python
import functools

import numpy as np

import jax
import jax.numpy as jnp
from jax import lax
from jax.experimental import pallas as pl
from jax.experimental.pallas import tpu as pltpu
from jax.sharding import PartitionSpec as P

F32 = jnp.float32
BF16 = jnp.bfloat16
TX, TY, TZ = 16, 32, 4
ROWS = TX * TY
COL = TZ * 512
PITCH = 40
GRID = 1024
HROWS = 112
CROWS = 6 * HROWS
TIKHONOV = 8.0
SCALE = 2.0**-8
PAIRS = [(0, 0), (0, 1), (0, 2), (1, 1), (1, 2), (2, 2)]
DOTS = [(0, 0), (0, 1), (0, 2), (0, 3), (1, 1), (1, 2), (1, 3), (2, 2), (2, 3)]


def voxel_factors():
    v = np.arange(512)
    coords = [(v // 64 + 0.5) / 8.0, (v // 8 % 8 + 0.5) / 8.0, (v % 8 + 0.5) / 8.0]
    return [(1.0 - t, t) for t in coords]


def hessian_table():
    s = voxel_factors()
    q = [(a * a, a * b, b * b) for a, b in s]
    table = np.zeros((HROWS, TZ, 512))
    for tj in range(3):
        for tl in range(3):
            for ti in range(3):
                t = (tj * 3 + tl) * 3 + ti
                for ez in range(TZ):
                    table[4 * t + ez, ez] = q[0][ti] * q[1][tj] * q[2][tl]
    table = np.concatenate([table, np.zeros((128 - HROWS, TZ, 512))])
    return np.ascontiguousarray(table.reshape(128, COL).T).astype(jnp.bfloat16)


def load_table():
    s = voxel_factors()
    table = np.zeros((32, TZ, 512), np.float32)
    for j in range(2):
        for l in range(2):
            for i in range(2):
                for ez in range(TZ):
                    table[(j * 2 + l) * 8 + i * 4 + ez, ez] = s[0][i] * s[1][j] * s[2][l]
    table = table.reshape(32, COL)
    high = table.astype(jnp.bfloat16)
    low = (table - high.astype(np.float32)).astype(jnp.bfloat16)
    both = np.concatenate([high, low, np.zeros((64, COL), high.dtype)], axis=0)
    return np.ascontiguousarray(both.T)


def edge_maps(low, high, xlo_lanes, xhi_lanes):
    ysend, ycoord = [], []
    for x in range(TX):
        for k in range(low):
            ysend.append(x * TY + TY - low + k)
            ycoord.append((x, k - low))
    for x in range(TX):
        for k in range(high):
            ysend.append(x * TY + k)
            ycoord.append((x, TY + k))
    lane_of = {c: n for n, c in enumerate(ycoord)}

    def strip(first, count, base):
        lanes, coord = [], []
        for x in range(first, first + count):
            for y in range(TY):
                lanes.append(x * TY + y)
                coord.append((x + base, y))
        for ys in (range(-low, 0), range(TY, TY + high)):
            for x in range(first, first + count):
                for y in ys:
                    lanes.append(ROWS + lane_of[(x, y)])
                    coord.append((x + base, y))
        return lanes, coord

    up, up_coord = strip(TX - low, low, -TX)
    down, down_coord = strip(0, high, TX)
    source = {}
    for x in range(TX):
        for y in range(TY):
            source[(x, y)] = x * TY + y
    for n, c in enumerate(ycoord):
        source[c] = ROWS + n
    for n, c in enumerate(up_coord):
        source[c] = ROWS + 128 + n
    for n, c in enumerate(down_coord):
        source[c] = ROWS + 128 + xlo_lanes + n
    grid = np.full((GRID,), -1)
    for (x, y), lane in source.items():
        grid[(x + 4) * PITCH + y + 4] = lane

    def row(values, lanes):
        out = np.full((1, lanes), -1, np.int32)
        out[0, : len(values)] = values
        return out

    xsend = np.concatenate([row(up, xlo_lanes), row(down, xhi_lanes)], axis=1)
    return row(ysend, 128), xsend, row(list(grid), GRID), low * TX


H_YSEND, H_XSEND, H_GRID, H_YLOW = edge_maps(3, 2, 128, 128)
L_YSEND, L_XSEND, L_GRID, L_YLOW = edge_maps(4, 3, 256, 128)
OWN_MAP = np.array(
    [[(x + 4) * PITCH + y + 4 for x in range(TX) for y in range(TY)]], np.int32
)


def lane_maps():
    position = np.arange(GRID)
    rows = np.full((8, GRID), -1, np.int32)
    rows[0] = H_GRID
    rows[1] = L_GRID
    rows[2] = position // PITCH - 4
    rows[3] = position % PITCH - 4
    rows[4, :512] = OWN_MAP
    rows[5, :128] = H_YSEND
    rows[5, 128:384] = np.where(H_XSEND < ROWS, H_XSEND, -1)
    rows[5, 384:640] = H_XSEND
    rows[6, :128] = L_YSEND
    rows[6, 128:512] = L_XSEND
    return rows


MAP = {
    "h_grid": (0, 0, 1024),
    "l_grid": (1, 0, 1024),
    "x": (2, 0, 1024),
    "y": (3, 0, 1024),
    "own": (4, 0, 512),
    "h_ysend": (5, 0, 128),
    "h_xown": (5, 128, 384),
    "h_xsend": (5, 384, 640),
    "l_ysend": (6, 0, 128),
    "l_xsend": (6, 128, 512),
}


def lane_map(maps_ref, name):
    row, first, last = MAP[name]
    return maps_ref[row : row + 1, first:last]


def onehot(index_row, depth):
    lanes = index_row.shape[1]
    rows = lax.broadcasted_iota(jnp.int32, (depth, lanes), 0)
    return jnp.where(rows == index_row, 1.0, 0.0).astype(BF16)


def select_lanes(value, choice, parts):
    pieces, rest = [], value
    for part in range(parts):
        pieces.append(rest.astype(BF16))
        rest = rest - pieces[-1].astype(F32)
    stacked = jnp.dot(jnp.concatenate(pieces, axis=0), choice, preferred_element_type=F32)
    rows = value.shape[0]
    total = stacked[:rows]
    for part in range(1, parts):
        total = total + stacked[part * rows : (part + 1) * rows]
    return total


def run_copies(sems, *moves):
    copies = [
        pltpu.make_async_copy(source, target, sems.at[k])
        for k, (source, target) in enumerate(moves)
    ]
    for copy in copies:
        copy.start()
    return copies


def pack_kernel(d_ref, up_ref, down_ref, last_ref, first_ref, ends, sems):
    copies = run_copies(
        sems,
        (d_ref.at[pl.ds(0, TX), pl.ds(TY // 8 - 1, 1)], ends.at[0]),
        (d_ref.at[pl.ds(0, TX), pl.ds(0, 1)], ends.at[1]),
        (d_ref.at[pl.ds(TX - 4, 4)], up_ref),
        (d_ref.at[pl.ds(0, 5)], down_ref),
    )
    row = lax.broadcasted_iota(jnp.int32, (64, 128), 0)
    pos = lax.broadcasted_iota(jnp.int32, (64, 128), 1)
    for k, (out_ref, at) in enumerate(((last_ref, 4), (first_ref, 0))):
        choice = jnp.where(pos == (row >> 2) * 8 + (row & 3) + at, 1.0, 0.0).astype(BF16)
        copies[k].wait()
        rows = ends[k].astype(F32).reshape(TX * 8, COL).astype(BF16)
        out_ref[...] = jnp.dot(choice, rows, preferred_element_type=F32).astype(BF16)
    copies[2].wait()
    copies[3].wait()


def corner_kernel(ylo_ref, yhi_ref, after_ref, up_ref, down_ref):
    up_ref[:16, :] = ylo_ref[48:, :]
    up_ref[16:, :] = yhi_ref[48:, :]
    down_ref[:24, :] = ylo_ref[:24, :]
    down_ref[24:, :] = yhi_ref[:24, :]


def hessian_kernel(g_ref, m_ref, table_ref, maps_ref, c_ref, cy_ref, cx_ref, mg_ref):
    chunk = 256

    def step(i, carry):
        rows = pl.ds(pl.multiple_of(i * chunk, chunk), chunk)
        mask = m_ref[rows, :].astype(F32).astype(BF16)
        for c in range(3):
            mg_ref[c, rows, :] = g_ref[c, rows, :] * mask
        for k, (c, d) in enumerate(PAIRS):
            x = mg_ref[c, rows, :] * g_ref[d, rows, :]
            sums = jnp.dot(x, table_ref[...], preferred_element_type=F32)
            c_ref[k * HROWS : (k + 1) * HROWS, rows] = jnp.transpose(sums, (1, 0))[:HROWS].astype(BF16)
        return carry

    lax.fori_loop(0, ROWS // chunk, step, 0)
    for name, ref in (("h_ysend", cy_ref), ("h_xown", cx_ref)):
        choice = onehot(lane_map(maps_ref, name), ROWS)
        ref[...] = jnp.dot(c_ref[...], choice, preferred_element_type=F32).astype(BF16)


def edge_kernel(
    l_ref, cx_ref, below_ref, above_ref, maps_ref, y_ref, up_ref, down_ref
):
    lane = lax.broadcasted_iota(jnp.int32, (1, 128), 1)
    ytile_c = jnp.where(lane < H_YLOW, below_ref[:CROWS, :], above_ref[:CROWS, :])
    ytile_l = jnp.where(lane < L_YLOW, below_ref[CROWS:, :], above_ref[CROWS:, :])
    y_ref[:CROWS, :] = ytile_c
    y_ref[CROWS:, :] = ytile_l
    sent = jnp.dot(ytile_c, onehot(lane_map(maps_ref, "h_xsend") - ROWS, 128), preferred_element_type=F32)
    sent = sent.astype(BF16) + cx_ref[...]
    up_ref[:CROWS, :] = sent[:, :128]
    down_ref[:CROWS, :] = sent[:, 128:]
    high = l_ref[...].astype(BF16)
    low = (l_ref[...] - high.astype(F32)).astype(BF16)
    source = jnp.concatenate([jnp.concatenate([high, low], axis=0), ytile_l], axis=1)
    sent = jnp.dot(
        source, onehot(lane_map(maps_ref, "l_xsend"), ROWS + 128), preferred_element_type=F32
    ).astype(BF16)
    up_ref[CROWS : CROWS + 192, :] = sent[:, :128]
    up_ref[CROWS + 192 :, :] = sent[:, 128:256]
    down_ref[CROWS:, :] = sent[:, 256:]


def grid_kernel(
    own_ref, l_ref, y_ref, maps_ref,
    out_ref, lout_ref, hchoice_ref, lchoice_ref, ochoice_ref,
):
    h_map, l_map = lane_map(maps_ref, "h_grid"), lane_map(maps_ref, "l_grid")
    source = jnp.concatenate([own_ref[...], y_ref[:CROWS, :]], axis=1)
    placed = jnp.dot(source, onehot(h_map, ROWS + 128), preferred_element_type=F32)
    for tile in range(GRID // 128):
        out_ref[tile] = placed[:, tile * 128 : (tile + 1) * 128]
    top = l_ref[...].astype(BF16)
    rest = (l_ref[...] - top.astype(F32)).astype(BF16)
    source = jnp.concatenate([jnp.concatenate([top, rest], axis=0), y_ref[CROWS:, :]], axis=1)
    placed = jnp.dot(source, onehot(l_map, ROWS + 128), preferred_element_type=F32)
    lout_ref[...] = placed[:96] + placed[96:]
    hchoice_ref[:, :256] = onehot(h_map[:, :256] - (ROWS + 128), 128)
    hchoice_ref[:, 256:] = onehot(h_map[:, 768:896] - (ROWS + 256), 128)
    lchoice_ref[...] = onehot(l_map - (ROWS + 128), 384)
    ochoice_ref[...] = onehot(lane_map(maps_ref, "own"), GRID)


def sample_slot(x, y):
    ymid = (y >= 0) & (y < TY)
    ylo = y < 0
    xmid = (x >= 0) & (x < TX)
    xlo = x < 0
    mid = jnp.where(
        xmid, x * TY + y, jnp.where(xlo, 512 + (x + 4) * TY + y, 672 + (x - TX) * TY + y)
    )
    left = jnp.where(xmid, 880 + x * 4, jnp.where(xlo, 640 + (x + 4) * 4, 832 + (x - TX) * 4))
    right = jnp.where(xmid, 944 + x * 4, jnp.where(xlo, 656 + (x + 4) * 4, 856 + (x - TX) * 4))
    return jnp.where(ymid, mid, jnp.where(ylo, left + y + 4, right + y - TY))


def slot_columns(o_ref, ez):
    layer = lax.broadcasted_iota(jnp.int32, (TX, TZ, TY), 1) == ez
    ox, oy = (jnp.sum(jnp.where(layer, o_ref[axis], 0), axis=1) for axis in range(2))
    x = lax.broadcasted_iota(jnp.int32, (TX, TY), 0) + ox
    y = lax.broadcasted_iota(jnp.int32, (TX, TY), 1) + oy
    near, far = sample_slot(x, y), sample_slot(x + 1, y)
    parts = jnp.concatenate([near >> 7, near & 127, far >> 7, far & 127], axis=1)
    row = lax.broadcasted_iota(jnp.int32, (ROWS, TX), 0)
    col = lax.broadcasted_iota(jnp.int32, (ROWS, TX), 1)
    spread = jnp.dot(
        jnp.where(row >> 5 == col, 1.0, 0.0).astype(BF16),
        parts.astype(F32).astype(BF16),
        preferred_element_type=F32,
    )
    row = lax.broadcasted_iota(jnp.int32, (ROWS, 128), 0)
    col = lax.broadcasted_iota(jnp.int32, (ROWS, 128), 1)
    spread = jnp.where(row & 31 == col & 31, spread, 0.0).astype(BF16)
    row = lax.broadcasted_iota(jnp.int32, (128, 512), 0)
    col = lax.broadcasted_iota(jnp.int32, (128, 512), 1)
    ones = jnp.where(row >> 5 == col >> 7, 1.0, 0.0).astype(BF16)
    out = jnp.dot(spread, ones, preferred_element_type=F32).astype(BF16)
    high = jnp.concatenate([out[:, :128], out[:, 256:384]], axis=0)
    low = jnp.concatenate([out[:, 128:256], out[:, 384:]], axis=0)
    return high, low


def slot_onehot(high, low, first):
    lane = lax.broadcasted_iota(jnp.int32, low.shape, 1).astype(F32).astype(BF16)
    zero = jnp.zeros(low.shape, BF16)
    hit = jnp.where(low == lane, jnp.ones(low.shape, BF16), zero)
    return jnp.concatenate([jnp.where(high == float(first + k), hit, zero) for k in range(4)], axis=1)


GHOST_AT = (0, 128, 160, 320, 368, 432)
GHOST_ROWS = (128, 32, 160, 48, 64, 64)


def blend(both, w):
    w = w.astype(F32)
    return w * both[:ROWS] + (1.0 - w) * both[ROWS:]


def own_samples_kernel(s_ref, w_ref, d_ref, o_ref, out_ref, after_ref):
    after_ref[...] = jnp.zeros_like(after_ref)
    for ez in range(TZ):
        lanes = slice(ez * 512, (ez + 1) * 512)
        high, low = slot_columns(o_ref, ez)
        both = jnp.dot(
            slot_onehot(high, low, 0), d_ref[:, lanes], preferred_element_type=F32
        )
        out_ref[:, lanes] = s_ref[:, lanes].astype(F32) - blend(both, w_ref[:, lanes])


def warp_kernel(
    t_ref, w_ref, mg_ref, p0, p1, p2, p3, p4, p5, o_ref, table_ref, maps_ref, cy_ref,
    l_ref, msg_ref, ghost,
):
    for at, rows, piece in zip(GHOST_AT, GHOST_ROWS, (p0, p1, p2, p3, p4, p5)):
        ghost[at : at + rows, :] = piece[...]
    ghost[496:512, :] = jnp.zeros((16, COL), BF16)
    sums = [None] * 3
    for ez in range(TZ):
        lanes = slice(ez * 512, (ez + 1) * 512)
        high, low = slot_columns(o_ref, ez)
        both = jnp.dot(
            slot_onehot(high, low, 4), ghost[:, lanes], preferred_element_type=F32
        )
        resid = (t_ref[:, lanes] - blend(both, w_ref[:, lanes])).astype(BF16)
        for c in range(3):
            part = jnp.dot(
                mg_ref[c, :, lanes] * resid, table_ref[lanes, :], preferred_element_type=F32
            )
            sums[c] = part if ez == 0 else sums[c] + part
    for c in range(3):
        part = jnp.transpose(sums[c], (1, 0))
        l_ref[c * 32 : (c + 1) * 32, :] = part[:32] + part[32:64]
    choice = onehot(lane_map(maps_ref, "l_ysend"), ROWS)
    loads = l_ref[...]
    top = loads.astype(BF16)
    rest = (loads - top.astype(F32)).astype(BF16)
    msg_ref[:CROWS, :] = cy_ref[...]
    msg_ref[CROWS:, :] = jnp.dot(
        jnp.concatenate([top, rest], axis=0), choice, preferred_element_type=F32
    ).astype(BF16)


def powers_kernel(
    edge_ref, lown_ref, xlo_ref, xhi_ref, hchoice_ref, lchoice_ref, maps_ref, ochoice_ref,
    hown_ref, v_ref, dots_ref, h_ref, us, fs,
):
    row = lax.broadcasted_iota(jnp.int32, (8, GRID), 0)
    beyond_x = (lane_map(maps_ref, "x") >= TX) & (edge_ref[0] == 1)
    beyond_y = (lane_map(maps_ref, "y") >= TY) & (edge_ref[1] == 1)
    live = jnp.where(beyond_x | beyond_y, 0.0, 1.0)

    def scatter(f):
        out = []
        for c in range(3):
            sums = []
            for l in range(2):
                both = f(0, l, c) + pltpu.roll(f(1, l, c), 1, axis=1)
                split = jnp.where(row < 4, both, pltpu.roll(both, PITCH, axis=1))
                sums.append(split + pltpu.roll(split, 4, axis=0))
            a, b = sums
            lower = a + jnp.where((row & 3) == 0, 0.0, pltpu.roll(b, 1, axis=0))
            upper = b + jnp.where((row & 3) == 3, 0.0, pltpu.roll(a, 7, axis=0))
            out.append((lower * live, upper * live))
        return out

    def apply(u):
        for i in range(2):
            for j in range(2):
                shift = i * PITCH + j
                for d in range(3):
                    for l in range(2):
                        value = u[d][l]
                        if shift:
                            value = pltpu.roll(value, GRID - shift, axis=1)
                        us[((i * 2 + j) * 3 + d) * 2 + l] = value

        def tile_step(tile, carry):
            lanes = pl.ds(pl.multiple_of(tile * 128, 128), 128)
            uu = [us[k, :, lanes] for k in range(24)]
            acc = {}
            for k, (c, d) in enumerate(PAIRS):
                for tj in range(3):
                    for tl in range(3):
                        for i in range(2):
                            at = k * HROWS + (tj * 3 + tl) * 12 + i * 4
                            h = h_ref[tile, at : at + 8, :]
                            for mj in range(2):
                                nj = tj - mj
                                if nj not in (0, 1):
                                    continue
                                for ml in range(2):
                                    nl = tl - ml
                                    if nl not in (0, 1):
                                        continue
                                    for out_c, in_d in {(c, d), (d, c)}:
                                        term = h * uu[((i * 2 + mj) * 3 + in_d) * 2 + ml]
                                        key = (nj * 2 + nl) * 3 + out_c
                                        acc[key] = term if key not in acc else acc[key] + term
            for key in range(12):
                fs[key, :, lanes] = acc[key] * SCALE
            return carry

        lax.fori_loop(0, GRID // 128, tile_step, 0)
        return scatter(lambda j, l, c: fs[(j * 2 + l) * 3 + c])

    placed = jnp.dot(xlo_ref[:CROWS, :], hchoice_ref[:, :256], preferred_element_type=F32)
    for tile in range(2):
        h_ref[tile] = hown_ref[tile] + placed[:, tile * 128 : (tile + 1) * 128]
    h_ref[6] = hown_ref[6] + jnp.dot(
        xhi_ref[:CROWS, :], hchoice_ref[:, 256:], preferred_element_type=F32
    )
    source = jnp.concatenate(
        [xlo_ref[CROWS : CROWS + 192, :], xlo_ref[CROWS + 192 :, :], xhi_ref[CROWS:, :]], axis=1
    )
    placed = jnp.dot(source, lchoice_ref[...], preferred_element_type=F32)
    loads = lown_ref[...] + placed[:96] + placed[96:]

    def load_rows(j, l, c):
        at = c * 32 + (j * 2 + l) * 8
        return loads[at : at + 8, :]

    vectors = [scatter(load_rows)]
    for _ in range(3):
        vectors.append(apply(vectors[-1]))
    pieces = []
    for vec in vectors:
        for lower, upper in vec:
            pieces.append(
                jnp.where(row < 4, lower, jnp.where(row == 4, pltpu.roll(upper, 1, axis=0), 0.0))
            )
    own = select_lanes(jnp.concatenate(pieces, axis=0), ochoice_ref[...], 3)
    v_ref[...] = own
    lane = lax.broadcasted_iota(jnp.int32, (1, 128), 1)
    dots = jnp.zeros((1, 128), F32)
    for k, (a, b) in enumerate(DOTS):
        product = own[a * 24 : a * 24 + 24] * own[b * 24 : b * 24 + 24]
        total = jnp.sum(jnp.sum(product, axis=0, keepdims=True), axis=1, keepdims=True)
        dots = jnp.where(lane == k, total, dots)
    dots_ref[...] = jnp.broadcast_to(dots, dots_ref.shape)


def combine_kernel(v_ref, dots_ref, x_ref, r_ref):
    total = jnp.sum(dots_ref[...], axis=0, keepdims=True)
    gram = {}
    for k, (a, b) in enumerate(DOTS):
        gram[(a, b)] = gram[(b, a)] = total[:, k : k + 1]

    def inner(p, q):
        out = None
        for a, pa in p.items():
            for b, qb in q.items():
                term = pa * qb * gram[(a, b)]
                out = term if out is None else out + term
        return out

    def add(p, q, factor):
        out = dict(p)
        for a, qa in q.items():
            term = factor * qa
            out[a] = out[a] + term if a in out else term
        return out

    one = jnp.ones((1, 1), F32)
    increment, resid, direction = {}, {0: one}, {0: one}
    norm_now = gram[(0, 0)]
    for sweep in range(3):
        image = {}
        for a, pa in direction.items():
            image[a] = image[a] + TIKHONOV * pa if a in image else TIKHONOV * pa
            image[a + 1] = pa * (1.0 / SCALE)
        step_size = norm_now / inner(direction, image)
        increment = add(increment, direction, step_size)
        resid = add(resid, image, -step_size)
        if sweep < 2:
            norm_next = inner(resid, resid)
            direction = add(resid, direction, norm_next / norm_now)
            norm_now = norm_next
    at_x = lax.broadcasted_iota(jnp.int32, (TX, ROWS), 1) >> 5 == lax.broadcasted_iota(
        jnp.int32, (TX, ROWS), 0
    )
    at_y = lax.broadcasted_iota(jnp.int32, (ROWS, TY), 0) & 31 == lax.broadcasted_iota(
        jnp.int32, (ROWS, TY), 1
    )
    pieces = []
    for coefs in (increment, resid):
        for c in range(3):
            out = None
            for k, coef in coefs.items():
                at = (k * 3 + c) * 8
                term = coef * v_ref[at : at + 8, :]
                out = term if out is None else out + term
            for z in range(TZ + 1):
                pieces.append(jnp.where(at_x, out[z : z + 1, :], 0.0))
    split = select_lanes(
        jnp.concatenate(pieces, axis=0), jnp.where(at_y, 1.0, 0.0).astype(BF16), 3
    )
    half = 3 * (TZ + 1) * TX
    x_ref[...] = split[:half]
    r_ref[...] = split[half:]


def whole(shape):
    return pl.BlockSpec(shape, lambda *_: (0,) * len(shape))


def call(kernel, outs, *args, name, us, scratch=(), vmem=8):
    return pl.pallas_call(
        kernel,
        out_shape=outs,
        in_specs=[pl.BlockSpec(memory_space=pltpu.VMEM)] * len(args),
        out_specs=jax.tree.map(lambda _: pl.BlockSpec(memory_space=pltpu.VMEM), outs),
        scratch_shapes=scratch,
        compiler_params=pltpu.CompilerParams(vmem_limit_bytes=vmem * 2**20),
        cost_estimate=cost(us),
        name=name,
    )(*args)


def struct(*shape, dtype=F32):
    return jax.ShapeDtypeStruct(shape, dtype)


def cost(us):
    return pl.CostEstimate(flops=int(us * 1.1e9), transcendentals=0, bytes_accessed=0)


def shifted(value, dx, dy):
    nx, ny = lax.axis_size("gx"), lax.axis_size("gy")
    pairs = []
    for x in range(nx):
        for y in range(ny):
            if 0 <= x + dx < nx and 0 <= y + dy < ny:
                pairs.append((x * ny + y, (x + dx) * ny + y + dy))
    return lax.ppermute(value, ("gx", "gy"), pairs)


def per_device(
    reference_scan, ref_gradient, deformed_scan, interp_weights, sample_mask, block_list, offsets
):
    scan = reference_scan.reshape(ROWS, COL)
    grad = ref_gradient.reshape(3, ROWS, COL)
    weights = interp_weights.reshape(ROWS, COL)
    mask = sample_mask.reshape(ROWS, COL)
    moved = deformed_scan.reshape(ROWS, COL)
    moves = jnp.transpose(offsets, (0, 1, 3, 2))
    maps = jnp.asarray(lane_maps())
    lanes = lambda rows: pl.BlockSpec((rows, 512), lambda i: (0, i))
    params = pltpu.CompilerParams(vmem_limit_bytes=8 * 2**20)
    bf = functools.partial(struct, dtype=BF16)

    vmem = pl.BlockSpec(memory_space=pltpu.VMEM)
    up, down, ylast, yfirst = pl.pallas_call(
        pack_kernel,
        out_shape=(bf(4, TY // 8, 8, COL), bf(5, TY // 8, 8, COL), bf(64, COL), bf(64, COL)),
        in_specs=[pl.BlockSpec(memory_space=pltpu.HBM)],
        out_specs=(vmem,) * 4,
        scratch_shapes=[
            pltpu.VMEM((2, TX, 1, 8, COL), BF16),
            pltpu.SemaphoreType.DMA((4,)),
        ],
        compiler_params=params,
        cost_estimate=cost(8),
        name="pack",
    )(deformed_scan.reshape(TX, TY // 8, 8, COL))
    xlo = shifted(up.reshape(128, COL), 1, 0)
    xhi = shifted(down.reshape(160, COL), -1, 0)
    moves, ylast = lax.optimization_barrier((moves, ylast))
    ylo, yhi = shifted(ylast, 0, 1), shifted(yfirst, 0, -1)
    partial_image, after = call(
        own_samples_kernel, (struct(ROWS, COL), struct(8, 128)), scan, weights, moved, moves,
        name="own_samples", us=5, vmem=14,
    )
    up, down = call(
        corner_kernel, (bf(32, COL), bf(48, COL)), ylo, yhi, after, name="corners", us=6
    )
    maps_late, up = lax.optimization_barrier((maps, up))
    clo, chi = shifted(up, 1, 0), shifted(down, -1, 0)

    coefs, coefs_y, coefs_x, masked = call(
        hessian_kernel,
        (bf(CROWS, ROWS), bf(CROWS, 128), bf(CROWS, 256), bf(3, ROWS, COL)),
        grad, mask, jnp.asarray(hessian_table()), maps_late,
        name="hessian", us=6,
    )
    loads, message = call(
        warp_kernel,
        (struct(96, ROWS), bf(CROWS + 192, 128)),
        partial_image, weights, masked, xlo, clo, xhi, chi, ylo, yhi, moves,
        jnp.asarray(load_table()), maps, coefs_y,
        name="warp", us=6, vmem=14, scratch=[pltpu.VMEM((512, COL), BF16)],
    )
    below, above = shifted(message, 0, 1), shifted(message, 0, -1)
    ytile, up, down = call(
        edge_kernel,
        (bf(CROWS + 192, 128), bf(CROWS + 384, 128), bf(CROWS + 192, 128)),
        loads, coefs_x, below, above, maps,
        name="edges", us=2,
    )
    ghosts = (shifted(up, 1, 0), shifted(down, -1, 0))
    stiffness, loads_grid, *choices = call(
        grid_kernel,
        (
            struct(GRID // 128, CROWS, 128), struct(96, GRID),
            bf(128, 384), bf(384, GRID), bf(GRID, ROWS),
        ),
        coefs, loads, ytile, maps,
        name="grid", us=3,
    )

    last = jnp.stack(
        [lax.axis_index("gx") == lax.axis_size("gx") - 1, lax.axis_index("gy") == lax.axis_size("gy") - 1]
    ).astype(jnp.int32)
    devices = lax.axis_size("gx") * lax.axis_size("gy")
    vectors, dots, _ = pl.pallas_call(
        powers_kernel,
        out_shape=(struct(96, ROWS), struct(devices, 128), struct(GRID // 128, CROWS, 128)),
        in_specs=[pl.BlockSpec(memory_space=pltpu.SMEM)] + [vmem] * 8,
        out_specs=(vmem,) * 3,
        scratch_shapes=[pltpu.VMEM((24, 8, GRID), F32), pltpu.VMEM((12, 8, GRID), F32)],
        input_output_aliases={8: 2},
        compiler_params=params,
        cost_estimate=cost(6),
        name="powers",
    )(
        last, loads_grid, *ghosts, choices[0], choices[1], maps, choices[2],
        stiffness,
    )
    dots = lax.all_to_all(dots, ("gx", "gy"), 0, 0, tiled=True)
    increment, resid = call(
        combine_kernel, (struct(240, TY), struct(240, TY)), vectors, dots, name="combine", us=3
    )
    return tuple(
        jnp.transpose(out.reshape(3, TZ + 1, TX, TY), (0, 2, 3, 1)) for out in (increment, resid)
    )


def solution(mesh):
    return jax.shard_map(
        per_device,
        mesh=mesh,
        in_specs=(
            P("gx", "gy", None),
            P(None, "gx", "gy", None),
            P("gx", "gy", None),
            P("gx", "gy", None),
            P("gx", "gy", None),
            P("gx", "gy"),
            P(None, "gx", "gy", None),
        ),
        out_specs=(P(None, "gx", "gy", None), P(None, "gx", "gy", None)),
        check_vma=False,
    )
```

```python
import functools

import numpy as np

import jax
import jax.numpy as jnp
from jax import lax
from jax.experimental import pallas as pl
from jax.experimental.pallas import tpu as pltpu
from jax.sharding import PartitionSpec as P

F32 = jnp.float32
BF16 = jnp.bfloat16
TX, TY, TZ = 16, 32, 4
ROWS = TX * TY
COL = TZ * 512
PITCH = 40
GRID = 1024
HROWS = 112
CROWS = 6 * HROWS
TIKHONOV = 8.0
SCALE = 2.0**-8
PAIRS = [(0, 0), (0, 1), (0, 2), (1, 1), (1, 2), (2, 2)]
DOTS = [(0, 0), (0, 1), (0, 2), (0, 3), (1, 1), (1, 2), (1, 3), (2, 2), (2, 3)]


def voxel_factors():
    v = np.arange(512)
    coords = [(v // 64 + 0.5) / 8.0, (v // 8 % 8 + 0.5) / 8.0, (v % 8 + 0.5) / 8.0]
    return [(1.0 - t, t) for t in coords]


def hessian_table():
    s = voxel_factors()
    q = [(a * a, a * b, b * b) for a, b in s]
    table = np.zeros((HROWS, TZ, 512))
    for tj in range(3):
        for tl in range(3):
            for ti in range(3):
                t = (tj * 3 + tl) * 3 + ti
                for ez in range(TZ):
                    table[4 * t + ez, ez] = q[0][ti] * q[1][tj] * q[2][tl]
    table = np.concatenate([table, np.zeros((128 - HROWS, TZ, 512))])
    return np.ascontiguousarray(table.reshape(128, COL).T).astype(jnp.bfloat16)


def load_table():
    s = voxel_factors()
    table = np.zeros((32, TZ, 512), np.float32)
    for j in range(2):
        for l in range(2):
            for i in range(2):
                for ez in range(TZ):
                    table[(j * 2 + l) * 8 + i * 4 + ez, ez] = s[0][i] * s[1][j] * s[2][l]
    table = table.reshape(32, COL)
    high = table.astype(jnp.bfloat16)
    low = (table - high.astype(np.float32)).astype(jnp.bfloat16)
    both = np.concatenate([high, low, np.zeros((64, COL), high.dtype)], axis=0)
    return np.ascontiguousarray(both.T)


SPARE = 112


def edge_maps(low, high, xlo_lanes, xhi_lanes):
    ysend, ycoord = [], []
    for x in range(TX):
        for k in range(low):
            ysend.append(x * TY + TY - low + k)
            ycoord.append((x, k - low))
    for x in range(TX):
        for k in range(high):
            ysend.append(x * TY + k)
            ycoord.append((x, TY + k))
    lane_of = {c: n for n, c in enumerate(ycoord)}

    def strip(first, count, base):
        lanes, coord = [], []
        for x in range(first, first + count):
            for y in range(TY):
                lanes.append(x * TY + y)
                coord.append((x + base, y))
        for ys in (range(-low, 0), range(TY, TY + high)):
            for x in range(first, first + count):
                for y in ys:
                    lanes.append(ROWS + lane_of[(x, y)])
                    coord.append((x + base, y))
        return lanes, coord

    up, up_coord = strip(TX - low, low, -TX)
    rest = max(len(up) - 128, 0)
    half = (rest + 1) // 2
    up_lanes = list(range(min(len(up), 128)))
    up_lanes += [128 + SPARE + k for k in range(min(half, rest))]
    up_lanes += [256 + SPARE + k for k in range(rest - half)]
    down, down_coord = strip(0, high, TX)
    source = {}
    for x in range(TX):
        for y in range(TY):
            source[(x, y)] = x * TY + y
    for n, c in enumerate(ycoord):
        source[c] = ROWS + n
    for n, c in zip(up_lanes, up_coord):
        source[c] = ROWS + 128 + n
    for n, c in enumerate(down_coord):
        source[c] = ROWS + 128 + xlo_lanes + n
    grid = np.full((GRID,), -1)
    for (x, y), lane in source.items():
        grid[(x + 4) * PITCH + y + 4] = lane

    def row(values, lanes):
        out = np.full((1, lanes), -1, np.int32)
        out[0, : len(values)] = values
        return out

    sent = np.full((1, xlo_lanes), -1, np.int32)
    sent[0, up_lanes] = up
    xsend = np.concatenate([sent, row(down, xhi_lanes)], axis=1)
    return row(ysend, 128), xsend, row(list(grid), GRID), low * TX


H_YSEND, H_XSEND, H_GRID, H_YLOW = edge_maps(3, 2, 128, 128)
L_YSEND, L_XSEND, L_GRID, L_YLOW = edge_maps(4, 3, 384, 128)
OWN_MAP = np.array(
    [[(x + 4) * PITCH + y + 4 for x in range(TX) for y in range(TY)]], np.int32
)


def lane_maps():
    position = np.arange(GRID)
    rows = np.full((8, GRID), -1, np.int32)
    rows[0] = H_GRID
    rows[1] = L_GRID
    rows[2] = position // PITCH - 4
    rows[3] = position % PITCH - 4
    rows[4, :512] = OWN_MAP
    rows[5, :128] = H_YSEND
    rows[5, 128:384] = np.where(H_XSEND < ROWS, H_XSEND, -1)
    rows[5, 384:640] = H_XSEND
    rows[6, :128] = L_YSEND
    rows[6, 128:640] = L_XSEND
    return rows


MAP = {
    "h_grid": (0, 0, 1024),
    "l_grid": (1, 0, 1024),
    "x": (2, 0, 1024),
    "y": (3, 0, 1024),
    "own": (4, 0, 512),
    "h_ysend": (5, 0, 128),
    "h_xown": (5, 128, 384),
    "h_xsend": (5, 384, 640),
    "l_ysend": (6, 0, 128),
    "l_xsend": (6, 128, 640),
}


def lane_map(maps_ref, name):
    row, first, last = MAP[name]
    return maps_ref[row : row + 1, first:last]


def onehot(index_row, depth):
    lanes = index_row.shape[1]
    rows = lax.broadcasted_iota(jnp.int32, (depth, lanes), 0)
    return jnp.where(rows == index_row, 1.0, 0.0).astype(BF16)


def select_lanes(value, choice, parts):
    pieces, rest = [], value
    for part in range(parts):
        pieces.append(rest.astype(BF16))
        rest = rest - pieces[-1].astype(F32)
    stacked = jnp.dot(jnp.concatenate(pieces, axis=0), choice, preferred_element_type=F32)
    rows = value.shape[0]
    total = stacked[:rows]
    for part in range(1, parts):
        total = total + stacked[part * rows : (part + 1) * rows]
    return total


def run_copies(sems, *moves):
    copies = [
        pltpu.make_async_copy(source, target, sems.at[k])
        for k, (source, target) in enumerate(moves)
    ]
    for copy in copies:
        copy.start()
    return copies


def either(flag, yes, no):
    return jnp.where(jnp.full(yes.shape, flag, jnp.int32) == 1, yes, no)


def pack_kernel(flags_ref, d_ref, xa_ref, xb_ref, ya_ref, yb_ref, ends, sems):
    odd_x, odd_y = flags_ref[2], flags_ref[3]
    high = TX - 5
    copies = run_copies(
        sems,
        (d_ref.at[pl.ds(0, TX), pl.ds(TY // 8 - 1, 1)], ends.at[0]),
        (d_ref.at[pl.ds(0, TX), pl.ds(0, 1)], ends.at[1]),
        (d_ref.at[pl.ds(high * odd_x, 5)], xa_ref),
        (d_ref.at[pl.ds(high - high * odd_x, 5)], xb_ref),
    )
    row = lax.broadcasted_iota(jnp.int32, (64, 128), 0)
    pos = lax.broadcasted_iota(jnp.int32, (64, 128), 1)
    found = []
    for k, at in enumerate((4, 0)):
        choice = jnp.where(pos == (row >> 2) * 8 + (row & 3) + at, 1.0, 0.0).astype(BF16)
        copies[k].wait()
        rows = ends[k].astype(F32).reshape(TX * 8, COL).astype(BF16)
        found.append(jnp.dot(choice, rows, preferred_element_type=F32))
    last, first = found
    ya_ref[...] = either(odd_y, last, first).astype(BF16)
    yb_ref[...] = either(odd_y, first, last).astype(BF16)
    copies[2].wait()
    copies[3].wait()


def corner_kernel(flags_ref, ya_ref, yb_ref, after_ref, a_ref, b_ref):
    for odd_x in range(2):
        for odd_y in range(2):

            @pl.when((flags_ref[2] == odd_x) & (flags_ref[3] == odd_y))
            def _():
                low, high = (yb_ref, ya_ref) if odd_y else (ya_ref, yb_ref)
                up, down = (a_ref, b_ref) if odd_x else (b_ref, a_ref)
                up[:24, :] = low[40:, :]
                up[24:, :] = high[40:, :]
                down[:24, :] = low[:24, :]
                down[24:, :] = high[:24, :]


def hessian_kernel(g_ref, m_ref, table_ref, maps_ref, c_ref, cy_ref, cx_ref, mg_ref):
    chunk = 256

    def step(i, carry):
        rows = pl.ds(pl.multiple_of(i * chunk, chunk), chunk)
        mask = m_ref[rows, :].astype(F32).astype(BF16)
        for c in range(3):
            mg_ref[c, rows, :] = g_ref[c, rows, :] * mask
        for k, (c, d) in enumerate(PAIRS):
            x = mg_ref[c, rows, :] * g_ref[d, rows, :]
            sums = jnp.dot(x, table_ref[...], preferred_element_type=F32)
            c_ref[k * HROWS : (k + 1) * HROWS, rows] = jnp.transpose(sums, (1, 0))[:HROWS].astype(BF16)
        return carry

    lax.fori_loop(0, ROWS // chunk, step, 0)
    for name, ref in (("h_ysend", cy_ref), ("h_xown", cx_ref)):
        choice = onehot(lane_map(maps_ref, name), ROWS)
        ref[...] = jnp.dot(c_ref[...], choice, preferred_element_type=F32).astype(BF16)


def edge_kernel(
    flags_ref, l_ref, cx_ref, ya_ref, yb_ref, maps_ref, y_ref, a_ref, b_ref
):
    lane = lax.broadcasted_iota(jnp.int32, (1, 128), 1)
    odd_y = jnp.full((1, 128), flags_ref[3], jnp.int32) == 1
    ytile_c = jnp.where((lane < H_YLOW) != odd_y, ya_ref[:CROWS, :], yb_ref[:CROWS, :])
    ytile_l = jnp.where((lane < L_YLOW) != odd_y, ya_ref[CROWS:, :], yb_ref[CROWS:, :])
    y_ref[:CROWS, :] = ytile_c
    y_ref[CROWS:, :] = ytile_l
    sent_c = jnp.dot(
        ytile_c, onehot(lane_map(maps_ref, "h_xsend") - ROWS, 128), preferred_element_type=F32
    )
    sent_c = sent_c.astype(BF16) + cx_ref[...]
    high = l_ref[...].astype(BF16)
    low = (l_ref[...] - high.astype(F32)).astype(BF16)
    source = jnp.concatenate([jnp.concatenate([high, low], axis=0), ytile_l], axis=1)
    sent = jnp.dot(
        source, onehot(lane_map(maps_ref, "l_xsend"), ROWS + 128), preferred_element_type=F32
    ).astype(BF16)

    def write(up_ref, down_ref):
        up_ref[:192, :] = sent_c[:192, :128] + sent[:, 128:256]
        up_ref[192:384, :] = sent_c[192:384, :128] + sent[:, 256:384]
        up_ref[384:CROWS, :] = sent_c[384:, :128]
        up_ref[CROWS:, :] = sent[:, :128]
        down_ref[:CROWS, :] = sent_c[:, 128:]
        down_ref[CROWS:, :] = sent[:, 384:]

    @pl.when(flags_ref[2] == 1)
    def _():
        write(a_ref, b_ref)

    @pl.when(flags_ref[2] == 0)
    def _():
        write(b_ref, a_ref)


def grid_kernel(
    own_ref, l_ref, y_ref, maps_ref,
    out_ref, lout_ref, hchoice_ref, lchoice_ref, ochoice_ref,
):
    h_map, l_map = lane_map(maps_ref, "h_grid"), lane_map(maps_ref, "l_grid")
    source = jnp.concatenate([own_ref[...], y_ref[:CROWS, :]], axis=1)
    placed = jnp.dot(source, onehot(h_map, ROWS + 128), preferred_element_type=F32)
    for tile in range(GRID // 128):
        out_ref[tile] = placed[:, tile * 128 : (tile + 1) * 128]
    top = l_ref[...].astype(BF16)
    rest = (l_ref[...] - top.astype(F32)).astype(BF16)
    source = jnp.concatenate([jnp.concatenate([top, rest], axis=0), y_ref[CROWS:, :]], axis=1)
    placed = jnp.dot(source, onehot(l_map, ROWS + 128), preferred_element_type=F32)
    lout_ref[...] = placed[:96] + placed[96:]
    hchoice_ref[:, :256] = onehot(h_map[:, :256] - (ROWS + 128), 128)
    hchoice_ref[:, 256:] = onehot(h_map[:, 768:896] - (ROWS + 256), 128)
    lchoice_ref[...] = onehot(l_map - (ROWS + 128), 512)
    ochoice_ref[...] = onehot(lane_map(maps_ref, "own"), GRID)


def sample_slot(x, y):
    ymid = (y >= 0) & (y < TY)
    ylo = y < 0
    xmid = (x >= 0) & (x < TX)
    xlo = x < 0
    mid = jnp.where(
        xmid, x * TY + y, jnp.where(xlo, 512 + (x + 4) * TY + y, 688 + (x - TX) * TY + y)
    )
    left = jnp.where(xmid, 896 + x * 4, jnp.where(xlo, 648 + (x + 4) * 4, 848 + (x - TX) * 4))
    right = jnp.where(xmid, 960 + x * 4, jnp.where(xlo, 672 + (x + 4) * 4, 872 + (x - TX) * 4))
    return jnp.where(ymid, mid, jnp.where(ylo, left + y + 4, right + y - TY))


def slot_columns(o_ref, ez):
    layer = lax.broadcasted_iota(jnp.int32, (TX, TZ, TY), 1) == ez
    ox, oy = (jnp.sum(jnp.where(layer, o_ref[axis], 0), axis=1) for axis in range(2))
    x = lax.broadcasted_iota(jnp.int32, (TX, TY), 0) + ox
    y = lax.broadcasted_iota(jnp.int32, (TX, TY), 1) + oy
    near, far = sample_slot(x, y), sample_slot(x + 1, y)
    parts = jnp.concatenate([near >> 7, near & 127, far >> 7, far & 127], axis=1)
    row = lax.broadcasted_iota(jnp.int32, (ROWS, TX), 0)
    col = lax.broadcasted_iota(jnp.int32, (ROWS, TX), 1)
    spread = jnp.dot(
        jnp.where(row >> 5 == col, 1.0, 0.0).astype(BF16),
        parts.astype(F32).astype(BF16),
        preferred_element_type=F32,
    )
    row = lax.broadcasted_iota(jnp.int32, (ROWS, 128), 0)
    col = lax.broadcasted_iota(jnp.int32, (ROWS, 128), 1)
    spread = jnp.where(row & 31 == col & 31, spread, 0.0).astype(BF16)
    row = lax.broadcasted_iota(jnp.int32, (128, 512), 0)
    col = lax.broadcasted_iota(jnp.int32, (128, 512), 1)
    ones = jnp.where(row >> 5 == col >> 7, 1.0, 0.0).astype(BF16)
    out = jnp.dot(spread, ones, preferred_element_type=F32).astype(BF16)
    high = jnp.concatenate([out[:, :128], out[:, 256:384]], axis=0)
    low = jnp.concatenate([out[:, 128:256], out[:, 384:]], axis=0)
    return high, low


def slot_onehot(high, low, first):
    lane = lax.broadcasted_iota(jnp.int32, low.shape, 1).astype(F32).astype(BF16)
    zero = jnp.zeros(low.shape, BF16)
    hit = jnp.where(low == lane, jnp.ones(low.shape, BF16), zero)
    return jnp.concatenate([jnp.where(high == float(first + k), hit, zero) for k in range(4)], axis=1)


def blend(both, w):
    w = w.astype(F32)
    return w * both[:ROWS] + (1.0 - w) * both[ROWS:]


def own_samples_kernel(s_ref, w_ref, d_ref, o_ref, out_ref, after_ref):
    after_ref[...] = jnp.zeros_like(after_ref)
    for ez in range(TZ):
        lanes = slice(ez * 512, (ez + 1) * 512)
        high, low = slot_columns(o_ref, ez)
        both = jnp.dot(
            slot_onehot(high, low, 0), d_ref[:, lanes], preferred_element_type=F32
        )
        out_ref[:, lanes] = s_ref[:, lanes].astype(F32) - blend(both, w_ref[:, lanes])


def warp_kernel(
    flags_ref, t_ref, w_ref, mg_ref, xa_ref, xb_ref, ca_ref, cb_ref, ya_ref, yb_ref, o_ref,
    table_ref, maps_ref, cy_ref,
    l_ref, msg_ref, ghost,
):
    for odd in range(2):

        @pl.when(flags_ref[2] == odd)
        def _():
            xlo, xhi = (xb_ref, xa_ref) if odd else (xa_ref, xb_ref)
            clo, chi = (cb_ref, ca_ref) if odd else (ca_ref, cb_ref)
            ghost[:128, :] = xlo[32:, :]
            ghost[128:176, :] = clo[...]
            ghost[176:336, :] = xhi[...]
            ghost[336:384, :] = chi[...]

        @pl.when(flags_ref[3] == odd)
        def _():
            ylo, yhi = (yb_ref, ya_ref) if odd else (ya_ref, yb_ref)
            ghost[384:448, :] = ylo[...]
            ghost[448:, :] = yhi[...]

    sums = [None] * 3
    for ez in range(TZ):
        lanes = slice(ez * 512, (ez + 1) * 512)
        high, low = slot_columns(o_ref, ez)
        both = jnp.dot(
            slot_onehot(high, low, 4), ghost[:, lanes], preferred_element_type=F32
        )
        resid = (t_ref[:, lanes] - blend(both, w_ref[:, lanes])).astype(BF16)
        for c in range(3):
            part = jnp.dot(
                mg_ref[c, :, lanes] * resid, table_ref[lanes, :], preferred_element_type=F32
            )
            sums[c] = part if ez == 0 else sums[c] + part
    for c in range(3):
        part = jnp.transpose(sums[c], (1, 0))
        l_ref[c * 32 : (c + 1) * 32, :] = part[:32] + part[32:64]
    choice = onehot(lane_map(maps_ref, "l_ysend"), ROWS)
    loads = l_ref[...]
    top = loads.astype(BF16)
    rest = (loads - top.astype(F32)).astype(BF16)
    msg_ref[:CROWS, :] = cy_ref[...]
    msg_ref[CROWS:, :] = jnp.dot(
        jnp.concatenate([top, rest], axis=0), choice, preferred_element_type=F32
    ).astype(BF16)


def powers_kernel(
    flags_ref, lown_ref, a_ref, b_ref, hchoice_ref, lchoice_ref, maps_ref, ochoice_ref,
    hown_ref, v_ref, dots_ref, h_ref, us, fs,
):
    row = lax.broadcasted_iota(jnp.int32, (8, GRID), 0)
    beyond_x = (lane_map(maps_ref, "x") >= TX) & (flags_ref[0] == 1)
    beyond_y = (lane_map(maps_ref, "y") >= TY) & (flags_ref[1] == 1)
    live = jnp.where(beyond_x | beyond_y, 0.0, 1.0)

    def scatter(f):
        out = []
        for c in range(3):
            sums = []
            for l in range(2):
                both = f(0, l, c) + pltpu.roll(f(1, l, c), 1, axis=1)
                split = jnp.where(row < 4, both, pltpu.roll(both, PITCH, axis=1))
                sums.append(split + pltpu.roll(split, 4, axis=0))
            a, b = sums
            lower = a + jnp.where((row & 3) == 0, 0.0, pltpu.roll(b, 1, axis=0))
            upper = b + jnp.where((row & 3) == 3, 0.0, pltpu.roll(a, 7, axis=0))
            out.append((lower * live, upper * live))
        return out

    def apply(u):
        for i in range(2):
            for j in range(2):
                shift = i * PITCH + j
                for d in range(3):
                    for l in range(2):
                        value = u[d][l]
                        if shift:
                            value = pltpu.roll(value, GRID - shift, axis=1)
                        us[((i * 2 + j) * 3 + d) * 2 + l] = value

        def tile_step(tile, carry):
            lanes = pl.ds(pl.multiple_of(tile * 128, 128), 128)
            uu = [us[k, :, lanes] for k in range(24)]
            acc = {}
            for k, (c, d) in enumerate(PAIRS):
                for tj in range(3):
                    for tl in range(3):
                        for i in range(2):
                            at = k * HROWS + (tj * 3 + tl) * 12 + i * 4
                            h = h_ref[tile, at : at + 8, :]
                            for mj in range(2):
                                nj = tj - mj
                                if nj not in (0, 1):
                                    continue
                                for ml in range(2):
                                    nl = tl - ml
                                    if nl not in (0, 1):
                                        continue
                                    for out_c, in_d in {(c, d), (d, c)}:
                                        term = h * uu[((i * 2 + mj) * 3 + in_d) * 2 + ml]
                                        key = (nj * 2 + nl) * 3 + out_c
                                        acc[key] = term if key not in acc else acc[key] + term
            for key in range(12):
                fs[key, :, lanes] = acc[key] * SCALE
            return carry

        lax.fori_loop(0, GRID // 128, tile_step, 0)
        return scatter(lambda j, l, c: fs[(j * 2 + l) * 3 + c])

    xlo = either(flags_ref[2], b_ref[...], a_ref[...])
    xhi = either(flags_ref[2], a_ref[...], b_ref[...])
    placed = jnp.dot(xlo[:CROWS, :], hchoice_ref[:, :256], preferred_element_type=F32)
    for tile in range(2):
        h_ref[tile] = hown_ref[tile] + placed[:, tile * 128 : (tile + 1) * 128]
    h_ref[6] = hown_ref[6] + jnp.dot(
        xhi[:CROWS, :], hchoice_ref[:, 256:], preferred_element_type=F32
    )
    source = jnp.concatenate(
        [xlo[CROWS:, :], xlo[:192, :], xlo[192:384, :], xhi[CROWS:, :]], axis=1
    )
    placed = jnp.dot(source, lchoice_ref[...], preferred_element_type=F32)
    loads = lown_ref[...] + placed[:96] + placed[96:]

    def load_rows(j, l, c):
        at = c * 32 + (j * 2 + l) * 8
        return loads[at : at + 8, :]

    vectors = [scatter(load_rows)]
    for _ in range(3):
        vectors.append(apply(vectors[-1]))
    pieces = []
    for vec in vectors:
        for lower, upper in vec:
            pieces.append(
                jnp.where(row < 4, lower, jnp.where(row == 4, pltpu.roll(upper, 1, axis=0), 0.0))
            )
    own = select_lanes(jnp.concatenate(pieces, axis=0), ochoice_ref[...], 3)
    v_ref[...] = own
    lane = lax.broadcasted_iota(jnp.int32, (1, 128), 1)
    dots = jnp.zeros((1, 128), F32)
    for k, (a, b) in enumerate(DOTS):
        product = own[a * 24 : a * 24 + 24] * own[b * 24 : b * 24 + 24]
        total = jnp.sum(jnp.sum(product, axis=0, keepdims=True), axis=1, keepdims=True)
        dots = jnp.where(lane == k, total, dots)
    dots_ref[...] = jnp.broadcast_to(dots, dots_ref.shape)


def combine_kernel(v_ref, dots_ref, x_ref, r_ref):
    total = jnp.sum(dots_ref[...], axis=0, keepdims=True)
    gram = {}
    for k, (a, b) in enumerate(DOTS):
        gram[(a, b)] = gram[(b, a)] = total[:, k : k + 1]

    def inner(p, q):
        out = None
        for a, pa in p.items():
            for b, qb in q.items():
                term = pa * qb * gram[(a, b)]
                out = term if out is None else out + term
        return out

    def add(p, q, factor):
        out = dict(p)
        for a, qa in q.items():
            term = factor * qa
            out[a] = out[a] + term if a in out else term
        return out

    one = jnp.ones((1, 1), F32)
    increment, resid, direction = {}, {0: one}, {0: one}
    norm_now = gram[(0, 0)]
    for sweep in range(3):
        image = {}
        for a, pa in direction.items():
            image[a] = image[a] + TIKHONOV * pa if a in image else TIKHONOV * pa
            image[a + 1] = pa * (1.0 / SCALE)
        step_size = norm_now / inner(direction, image)
        increment = add(increment, direction, step_size)
        resid = add(resid, image, -step_size)
        if sweep < 2:
            norm_next = inner(resid, resid)
            direction = add(resid, direction, norm_next / norm_now)
            norm_now = norm_next
    at_x = lax.broadcasted_iota(jnp.int32, (TX, ROWS), 1) >> 5 == lax.broadcasted_iota(
        jnp.int32, (TX, ROWS), 0
    )
    at_y = lax.broadcasted_iota(jnp.int32, (ROWS, TY), 0) & 31 == lax.broadcasted_iota(
        jnp.int32, (ROWS, TY), 1
    )
    pieces = []
    for coefs in (increment, resid):
        for c in range(3):
            out = None
            for k, coef in coefs.items():
                at = (k * 3 + c) * 8
                term = coef * v_ref[at : at + 8, :]
                out = term if out is None else out + term
            for z in range(TZ + 1):
                pieces.append(jnp.where(at_x, out[z : z + 1, :], 0.0))
    split = select_lanes(
        jnp.concatenate(pieces, axis=0), jnp.where(at_y, 1.0, 0.0).astype(BF16), 3
    )
    half = 3 * (TZ + 1) * TX
    x_ref[...] = split[:half]
    r_ref[...] = split[half:]


def whole(shape):
    return pl.BlockSpec(shape, lambda *_: (0,) * len(shape))


def call(kernel, outs, *args, name, us, scratch=(), vmem=8, flags=None):
    operands = args if flags is None else (flags, *args)
    scalars = [] if flags is None else [pl.BlockSpec(memory_space=pltpu.SMEM)]
    return pl.pallas_call(
        kernel,
        out_shape=outs,
        in_specs=scalars + [pl.BlockSpec(memory_space=pltpu.VMEM)] * len(args),
        out_specs=jax.tree.map(lambda _: pl.BlockSpec(memory_space=pltpu.VMEM), outs),
        scratch_shapes=scratch,
        compiler_params=pltpu.CompilerParams(vmem_limit_bytes=vmem * 2**20),
        cost_estimate=cost(us),
        name=name,
    )(*operands)


def struct(*shape, dtype=F32):
    return jax.ShapeDtypeStruct(shape, dtype)


def cost(us):
    return pl.CostEstimate(flops=int(us * 1.1e9), transcendentals=0, bytes_accessed=0)


def swapped(value, axis, first):
    size = lax.axis_size(axis)
    pairs = []
    for low in range(1 if first else 0, size - 1, 2):
        pairs += [(low, low + 1), (low + 1, low)]
    return lax.ppermute(value, axis, pairs)


def per_device(
    reference_scan, ref_gradient, deformed_scan, interp_weights, sample_mask, block_list, offsets
):
    scan = reference_scan.reshape(ROWS, COL)
    grad = ref_gradient.reshape(3, ROWS, COL)
    weights = interp_weights.reshape(ROWS, COL)
    mask = sample_mask.reshape(ROWS, COL)
    moved = deformed_scan.reshape(ROWS, COL)
    moves = jnp.transpose(offsets, (0, 1, 3, 2))
    maps = jnp.asarray(lane_maps())
    lanes = lambda rows: pl.BlockSpec((rows, 512), lambda i: (0, i))
    params = pltpu.CompilerParams(vmem_limit_bytes=8 * 2**20)
    bf = functools.partial(struct, dtype=BF16)

    vmem = pl.BlockSpec(memory_space=pltpu.VMEM)
    at_x, at_y = lax.axis_index("gx"), lax.axis_index("gy")
    flags = jnp.stack(
        [
            at_x == lax.axis_size("gx") - 1,
            at_y == lax.axis_size("gy") - 1,
            at_x % 2 == 1,
            at_y % 2 == 1,
        ]
    ).astype(jnp.int32)
    xa, xb, ya, yb = pl.pallas_call(
        pack_kernel,
        out_shape=(bf(5, TY // 8, 8, COL), bf(5, TY // 8, 8, COL), bf(64, COL), bf(64, COL)),
        in_specs=[pl.BlockSpec(memory_space=pltpu.SMEM), pl.BlockSpec(memory_space=pltpu.HBM)],
        out_specs=(vmem,) * 4,
        scratch_shapes=[
            pltpu.VMEM((2, TX, 1, 8, COL), BF16),
            pltpu.SemaphoreType.DMA((4,)),
        ],
        compiler_params=params,
        cost_estimate=cost(8),
        name="pack",
    )(flags, deformed_scan.reshape(TX, TY // 8, 8, COL))
    xa = swapped(xa.reshape(160, COL), "gx", True)
    xb = swapped(xb.reshape(160, COL), "gx", False)
    moves, ya = lax.optimization_barrier((moves, ya))
    ya, yb = swapped(ya, "gy", True), swapped(yb, "gy", False)
    partial_image, after = call(
        own_samples_kernel, (struct(ROWS, COL), struct(8, 128)), scan, weights, moved, moves,
        name="own_samples", us=2, vmem=14,
    )
    ca, cb = call(
        corner_kernel, (bf(48, COL), bf(48, COL)), ya, yb, after, name="corners", us=1,
        flags=flags,
    )
    maps_late, ca = lax.optimization_barrier((maps, ca))
    ca, cb = swapped(ca, "gx", True), swapped(cb, "gx", False)

    coefs, coefs_y, coefs_x, masked = call(
        hessian_kernel,
        (bf(CROWS, ROWS), bf(CROWS, 128), bf(CROWS, 256), bf(3, ROWS, COL)),
        grad, mask, jnp.asarray(hessian_table()), maps_late,
        name="hessian", us=1,
    )
    loads, message = call(
        warp_kernel,
        (struct(96, ROWS), bf(CROWS + 192, 128)),
        partial_image, weights, masked, xa, xb, ca, cb, ya, yb, moves,
        jnp.asarray(load_table()), maps, coefs_y,
        name="warp", us=6, vmem=14, flags=flags, scratch=[pltpu.VMEM((512, COL), BF16)],
    )
    ma, mb = swapped(message, "gy", True), swapped(message, "gy", False)
    ytile, ga, gb = call(
        edge_kernel, (bf(CROWS + 192, 128),) * 3, loads, coefs_x, ma, mb, maps,
        name="edges", us=2, flags=flags,
    )
    ghosts = (swapped(ga, "gx", True), swapped(gb, "gx", False))
    stiffness, loads_grid, *choices = call(
        grid_kernel,
        (
            struct(GRID // 128, CROWS, 128), struct(96, GRID),
            bf(128, 384), bf(512, GRID), bf(GRID, ROWS),
        ),
        coefs, loads, ytile, maps,
        name="grid", us=3,
    )

    devices = lax.axis_size("gx") * lax.axis_size("gy")
    vectors, dots, _ = pl.pallas_call(
        powers_kernel,
        out_shape=(struct(96, ROWS), struct(devices, 128), struct(GRID // 128, CROWS, 128)),
        in_specs=[pl.BlockSpec(memory_space=pltpu.SMEM)] + [vmem] * 8,
        out_specs=(vmem,) * 3,
        scratch_shapes=[pltpu.VMEM((24, 8, GRID), F32), pltpu.VMEM((12, 8, GRID), F32)],
        input_output_aliases={8: 2},
        compiler_params=params,
        cost_estimate=cost(6),
        name="powers",
    )(
        flags, loads_grid, *ghosts, choices[0], choices[1], maps, choices[2],
        stiffness,
    )
    dots = lax.all_to_all(dots, ("gx", "gy"), 0, 0, tiled=True)
    increment, resid = call(
        combine_kernel, (struct(240, TY), struct(240, TY)), vectors, dots, name="combine", us=3
    )
    return tuple(
        jnp.transpose(out.reshape(3, TZ + 1, TX, TY), (0, 2, 3, 1)) for out in (increment, resid)
    )


def solution(mesh):
    return jax.shard_map(
        per_device,
        mesh=mesh,
        in_specs=(
            P("gx", "gy", None),
            P(None, "gx", "gy", None),
            P("gx", "gy", None),
            P("gx", "gy", None),
            P("gx", "gy", None),
            P("gx", "gy"),
            P(None, "gx", "gy", None),
        ),
        out_specs=(P(None, "gx", "gy", None), P(None, "gx", "gy", None)),
        check_vma=False,
    )
```

```python
import functools

import numpy as np

import jax
import jax.numpy as jnp
from jax import lax
from jax.experimental import pallas as pl
from jax.experimental.pallas import tpu as pltpu
from jax.sharding import PartitionSpec as P

F32 = jnp.float32
BF16 = jnp.bfloat16
TX, TY, TZ = 16, 32, 4
ROWS = TX * TY
COL = TZ * 512
PITCH = 40
GRID = 1024
HROWS = 112
CROWS = 6 * HROWS
TIKHONOV = 8.0
SCALE = 2.0**-8
PAIRS = [(0, 0), (0, 1), (0, 2), (1, 1), (1, 2), (2, 2)]
DOTS = [(0, 0), (0, 1), (0, 2), (0, 3), (1, 1), (1, 2), (1, 3), (2, 2), (2, 3)]


def voxel_factors():
    v = np.arange(512)
    coords = [(v // 64 + 0.5) / 8.0, (v // 8 % 8 + 0.5) / 8.0, (v % 8 + 0.5) / 8.0]
    return [(1.0 - t, t) for t in coords]


def hessian_table():
    s = voxel_factors()
    q = [(a * a, a * b, b * b) for a, b in s]
    table = np.zeros((HROWS, TZ, 512))
    for tj in range(3):
        for tl in range(3):
            for ti in range(3):
                t = (tj * 3 + tl) * 3 + ti
                for ez in range(TZ):
                    table[4 * t + ez, ez] = q[0][ti] * q[1][tj] * q[2][tl]
    table = np.concatenate([table, np.zeros((128 - HROWS, TZ, 512))])
    return np.ascontiguousarray(table.reshape(128, COL).T).astype(jnp.bfloat16)


def load_table():
    s = voxel_factors()
    table = np.zeros((32, TZ, 512), np.float32)
    for j in range(2):
        for l in range(2):
            for i in range(2):
                for ez in range(TZ):
                    table[(j * 2 + l) * 8 + i * 4 + ez, ez] = s[0][i] * s[1][j] * s[2][l]
    table = table.reshape(32, COL)
    high = table.astype(jnp.bfloat16)
    low = (table - high.astype(np.float32)).astype(jnp.bfloat16)
    both = np.concatenate([high, low, np.zeros((64, COL), high.dtype)], axis=0)
    return np.ascontiguousarray(both.T)


def edge_maps(low, high, xlo_lanes, xhi_lanes):
    ysend, ycoord = [], []
    for x in range(TX):
        for k in range(low):
            ysend.append(x * TY + TY - low + k)
            ycoord.append((x, k - low))
    for x in range(TX):
        for k in range(high):
            ysend.append(x * TY + k)
            ycoord.append((x, TY + k))
    lane_of = {c: n for n, c in enumerate(ycoord)}

    def strip(first, count, base):
        lanes, coord = [], []
        for x in range(first, first + count):
            for y in range(TY):
                lanes.append(x * TY + y)
                coord.append((x + base, y))
        for ys in (range(-low, 0), range(TY, TY + high)):
            for x in range(first, first + count):
                for y in ys:
                    lanes.append(ROWS + lane_of[(x, y)])
                    coord.append((x + base, y))
        return lanes, coord

    up, up_coord = strip(TX - low, low, -TX)
    up_lanes = list(range(len(up)))
    down, down_coord = strip(0, high, TX)
    source = {}
    for x in range(TX):
        for y in range(TY):
            source[(x, y)] = x * TY + y
    for n, c in enumerate(ycoord):
        source[c] = ROWS + n
    for n, c in zip(up_lanes, up_coord):
        source[c] = ROWS + 128 + n
    for n, c in enumerate(down_coord):
        source[c] = ROWS + 128 + xlo_lanes + n
    grid = np.full((GRID,), -1)
    for (x, y), lane in source.items():
        grid[(x + 4) * PITCH + y + 4] = lane

    def row(values, lanes):
        out = np.full((1, lanes), -1, np.int32)
        out[0, : len(values)] = values
        return out

    sent = np.full((1, xlo_lanes), -1, np.int32)
    sent[0, up_lanes] = up
    xsend = np.concatenate([sent, row(down, xhi_lanes)], axis=1)
    return row(ysend, 128), xsend, row(list(grid), GRID), low * TX


H_YSEND, H_XSEND, H_GRID, H_YLOW = edge_maps(3, 2, 128, 128)
L_YSEND, L_XSEND, L_GRID, L_YLOW = edge_maps(4, 3, 256, 128)
OWN_MAP = np.array(
    [[(x + 4) * PITCH + y + 4 for x in range(TX) for y in range(TY)]], np.int32
)


def lane_maps():
    position = np.arange(GRID)
    rows = np.full((8, GRID), -1, np.int32)
    rows[0] = H_GRID
    rows[1] = L_GRID
    rows[2] = position // PITCH - 4
    rows[3] = position % PITCH - 4
    rows[4, :512] = OWN_MAP
    rows[5, :128] = H_YSEND
    rows[5, 128:384] = np.where(H_XSEND < ROWS, H_XSEND, -1)
    rows[5, 384:640] = H_XSEND
    rows[6, :128] = L_YSEND
    rows[6, 128:512] = L_XSEND
    return rows


MAP = {
    "h_grid": (0, 0, 1024),
    "l_grid": (1, 0, 1024),
    "x": (2, 0, 1024),
    "y": (3, 0, 1024),
    "own": (4, 0, 512),
    "h_ysend": (5, 0, 128),
    "h_xown": (5, 128, 384),
    "h_xsend": (5, 384, 640),
    "l_ysend": (6, 0, 128),
    "l_xsend": (6, 128, 512),
}


def lane_map(maps_ref, name):
    row, first, last = MAP[name]
    return maps_ref[row : row + 1, first:last]


def onehot(index_row, depth):
    lanes = index_row.shape[1]
    rows = lax.broadcasted_iota(jnp.int32, (depth, lanes), 0)
    return jnp.where(rows == index_row, 1.0, 0.0).astype(BF16)


def select_lanes(value, choice, parts):
    pieces, rest = [], value
    for part in range(parts):
        pieces.append(rest.astype(BF16))
        rest = rest - pieces[-1].astype(F32)
    stacked = jnp.dot(jnp.concatenate(pieces, axis=0), choice, preferred_element_type=F32)
    rows = value.shape[0]
    total = stacked[:rows]
    for part in range(1, parts):
        total = total + stacked[part * rows : (part + 1) * rows]
    return total


def run_copies(sems, *moves):
    copies = [
        pltpu.make_async_copy(source, target, sems.at[k])
        for k, (source, target) in enumerate(moves)
    ]
    for copy in copies:
        copy.start()
    return copies


def either(flag, yes, no):
    return jnp.where(jnp.full(yes.shape, flag, jnp.int32) == 1, yes, no)


def pack_kernel(flags_ref, d_ref, xa_ref, xb_ref, ya_ref, yb_ref, ends, sems):
    odd_x, odd_y = flags_ref[2], flags_ref[3]
    high = TX - 5
    copies = run_copies(
        sems,
        (d_ref.at[pl.ds(0, TX), pl.ds(TY // 8 - 1, 1)], ends.at[0]),
        (d_ref.at[pl.ds(0, TX), pl.ds(0, 1)], ends.at[1]),
        (d_ref.at[pl.ds(high * odd_x, 5)], xa_ref),
        (d_ref.at[pl.ds(high - high * odd_x, 5)], xb_ref),
    )
    row = lax.broadcasted_iota(jnp.int32, (64, 128), 0)
    pos = lax.broadcasted_iota(jnp.int32, (64, 128), 1)
    found = []
    for k, at in enumerate((4, 0)):
        choice = jnp.where(pos == (row >> 2) * 8 + (row & 3) + at, 1.0, 0.0).astype(BF16)
        copies[k].wait()
        rows = ends[k].astype(F32).reshape(TX * 8, COL).astype(BF16)
        found.append(jnp.dot(choice, rows, preferred_element_type=F32))
    last, first = found
    ya_ref[...] = either(odd_y, last, first).astype(BF16)
    yb_ref[...] = either(odd_y, first, last).astype(BF16)
    copies[2].wait()
    copies[3].wait()


def corner_kernel(flags_ref, ya_ref, yb_ref, after_ref, a_ref, b_ref):
    for odd_x in range(2):
        for odd_y in range(2):

            @pl.when((flags_ref[2] == odd_x) & (flags_ref[3] == odd_y))
            def _():
                low, high = (yb_ref, ya_ref) if odd_y else (ya_ref, yb_ref)
                up, down = (a_ref, b_ref) if odd_x else (b_ref, a_ref)
                up[:24, :] = low[40:, :]
                up[24:, :] = high[40:, :]
                down[:24, :] = low[:24, :]
                down[24:, :] = high[:24, :]


def hessian_kernel(g_ref, m_ref, table_ref, maps_ref, c_ref, cy_ref, cx_ref, mg_ref):
    chunk = 256

    def step(i, carry):
        rows = pl.ds(pl.multiple_of(i * chunk, chunk), chunk)
        mask = m_ref[rows, :].astype(F32).astype(BF16)
        for c in range(3):
            mg_ref[c, rows, :] = g_ref[c, rows, :] * mask
        for k, (c, d) in enumerate(PAIRS):
            x = mg_ref[c, rows, :] * g_ref[d, rows, :]
            sums = jnp.dot(x, table_ref[...], preferred_element_type=F32)
            c_ref[k * HROWS : (k + 1) * HROWS, rows] = jnp.transpose(sums, (1, 0))[:HROWS].astype(BF16)
        return carry

    lax.fori_loop(0, ROWS // chunk, step, 0)
    for name, ref in (("h_ysend", cy_ref), ("h_xown", cx_ref)):
        choice = onehot(lane_map(maps_ref, name), ROWS)
        ref[...] = jnp.dot(c_ref[...], choice, preferred_element_type=F32).astype(BF16)


def y_tile(flags_ref, a_ref, b_ref, ylow):
    lane = lax.broadcasted_iota(jnp.int32, (1, 128), 1)
    odd_y = jnp.full((1, 128), flags_ref[3], jnp.int32) == 1
    return jnp.where((lane < ylow) != odd_y, a_ref[...], b_ref[...])


def store_pair(flags_ref, up, down, a_ref, b_ref):
    @pl.when(flags_ref[2] == 1)
    def _():
        a_ref[...] = up
        b_ref[...] = down

    @pl.when(flags_ref[2] == 0)
    def _():
        a_ref[...] = down
        b_ref[...] = up


def hessian_edge_kernel(flags_ref, cx_ref, ya_ref, yb_ref, maps_ref, y_ref, a_ref, b_ref):
    ytile = y_tile(flags_ref, ya_ref, yb_ref, H_YLOW)
    y_ref[...] = ytile
    choice = onehot(lane_map(maps_ref, "h_xsend") - ROWS, 128)
    sent = jnp.dot(ytile, choice, preferred_element_type=F32).astype(BF16) + cx_ref[...]
    store_pair(flags_ref, sent[:, :128], sent[:, 128:], a_ref, b_ref)


def load_edge_kernel(flags_ref, l_ref, ya_ref, yb_ref, maps_ref, y_ref, a_ref, b_ref):
    ytile = y_tile(flags_ref, ya_ref, yb_ref, L_YLOW)
    y_ref[...] = ytile
    high = l_ref[...].astype(BF16)
    low = (l_ref[...] - high.astype(F32)).astype(BF16)
    source = jnp.concatenate([jnp.concatenate([high, low], axis=0), ytile], axis=1)
    sent = jnp.dot(
        source, onehot(lane_map(maps_ref, "l_xsend"), ROWS + 128), preferred_element_type=F32
    ).astype(BF16)
    up = jnp.concatenate([sent[:, :128], sent[:, 128:256]], axis=0)
    down = jnp.concatenate([sent[:, 256:], jnp.zeros((192, 128), BF16)], axis=0)
    store_pair(flags_ref, up, down, a_ref, b_ref)


def grid_kernel(
    own_ref, l_ref, yh_ref, yl_ref, maps_ref,
    out_ref, lout_ref, hchoice_ref, lchoice_ref, ochoice_ref,
):
    h_map, l_map = lane_map(maps_ref, "h_grid"), lane_map(maps_ref, "l_grid")
    source = jnp.concatenate([own_ref[...], yh_ref[...]], axis=1)
    placed = jnp.dot(source, onehot(h_map, ROWS + 128), preferred_element_type=F32)
    for tile in range(GRID // 128):
        out_ref[tile] = placed[:, tile * 128 : (tile + 1) * 128]
    top = l_ref[...].astype(BF16)
    rest = (l_ref[...] - top.astype(F32)).astype(BF16)
    source = jnp.concatenate([jnp.concatenate([top, rest], axis=0), yl_ref[...]], axis=1)
    placed = jnp.dot(source, onehot(l_map, ROWS + 128), preferred_element_type=F32)
    lout_ref[...] = placed[:96] + placed[96:]
    hchoice_ref[:, :256] = onehot(h_map[:, :256] - (ROWS + 128), 128)
    hchoice_ref[:, 256:] = onehot(h_map[:, 768:896] - (ROWS + 256), 128)
    lchoice_ref[...] = onehot(l_map - (ROWS + 128), 384)
    ochoice_ref[...] = onehot(lane_map(maps_ref, "own"), GRID)


def sample_slot(x, y):
    ymid = (y >= 0) & (y < TY)
    ylo = y < 0
    xmid = (x >= 0) & (x < TX)
    xlo = x < 0
    mid = jnp.where(
        xmid, x * TY + y, jnp.where(xlo, 512 + (x + 4) * TY + y, 688 + (x - TX) * TY + y)
    )
    left = jnp.where(xmid, 896 + x * 4, jnp.where(xlo, 648 + (x + 4) * 4, 848 + (x - TX) * 4))
    right = jnp.where(xmid, 960 + x * 4, jnp.where(xlo, 672 + (x + 4) * 4, 872 + (x - TX) * 4))
    return jnp.where(ymid, mid, jnp.where(ylo, left + y + 4, right + y - TY))


def slot_columns(o_ref, ez):
    layer = lax.broadcasted_iota(jnp.int32, (TX, TZ, TY), 1) == ez
    ox, oy = (jnp.sum(jnp.where(layer, o_ref[axis], 0), axis=1) for axis in range(2))
    x = lax.broadcasted_iota(jnp.int32, (TX, TY), 0) + ox
    y = lax.broadcasted_iota(jnp.int32, (TX, TY), 1) + oy
    near, far = sample_slot(x, y), sample_slot(x + 1, y)
    parts = jnp.concatenate([near >> 7, near & 127, far >> 7, far & 127], axis=1)
    row = lax.broadcasted_iota(jnp.int32, (ROWS, TX), 0)
    col = lax.broadcasted_iota(jnp.int32, (ROWS, TX), 1)
    spread = jnp.dot(
        jnp.where(row >> 5 == col, 1.0, 0.0).astype(BF16),
        parts.astype(F32).astype(BF16),
        preferred_element_type=F32,
    )
    row = lax.broadcasted_iota(jnp.int32, (ROWS, 128), 0)
    col = lax.broadcasted_iota(jnp.int32, (ROWS, 128), 1)
    spread = jnp.where(row & 31 == col & 31, spread, 0.0).astype(BF16)
    row = lax.broadcasted_iota(jnp.int32, (128, 512), 0)
    col = lax.broadcasted_iota(jnp.int32, (128, 512), 1)
    ones = jnp.where(row >> 5 == col >> 7, 1.0, 0.0).astype(BF16)
    out = jnp.dot(spread, ones, preferred_element_type=F32).astype(BF16)
    high = jnp.concatenate([out[:, :128], out[:, 256:384]], axis=0)
    low = jnp.concatenate([out[:, 128:256], out[:, 384:]], axis=0)
    return high, low


def slot_onehot(high, low, first, last):
    lane = lax.broadcasted_iota(jnp.int32, low.shape, 1).astype(F32).astype(BF16)
    zero = jnp.zeros(low.shape, BF16)
    hit = jnp.where(low == lane, jnp.ones(low.shape, BF16), zero)
    return jnp.concatenate([jnp.where(high == float(first + k), hit, zero) for k in range(last - first)], axis=1)


def end_rows(value):
    return jnp.concatenate([value[:128], value[352:640], value[864:]], axis=0)


def middle_rows(value):
    return jnp.concatenate([value[128:352], value[640:864]], axis=0)


def blend(both, w):
    w = w.astype(F32)
    return w * both[:ROWS] + (1.0 - w) * both[ROWS:]


def own_samples_kernel(s_ref, w_ref, d_ref, o_ref, out_ref, after_ref):
    after_ref[...] = jnp.zeros_like(after_ref)
    for ez in range(TZ):
        lanes = slice(ez * 512, (ez + 1) * 512)
        high, low = slot_columns(o_ref, ez)
        both = jnp.dot(
            slot_onehot(high, low, 0, 4), d_ref[:, lanes], preferred_element_type=F32
        )
        out_ref[:, lanes] = s_ref[:, lanes].astype(F32) - blend(both, w_ref[:, lanes])


def warp_kernel(
    flags_ref, t_ref, w_ref, mg_ref, xa_ref, xb_ref, ca_ref, cb_ref, ya_ref, yb_ref, o_ref,
    table_ref, maps_ref,
    l_ref, msg_ref, ghost,
):
    for odd in range(2):

        @pl.when(flags_ref[2] == odd)
        def _():
            xlo, xhi = (xb_ref, xa_ref) if odd else (xa_ref, xb_ref)
            clo, chi = (cb_ref, ca_ref) if odd else (ca_ref, cb_ref)
            ghost[:128, :] = xlo[32:, :]
            ghost[128:176, :] = clo[...]
            ghost[176:336, :] = xhi[...]
            ghost[336:384, :] = chi[...]

        @pl.when(flags_ref[3] == odd)
        def _():
            ylo, yhi = (yb_ref, ya_ref) if odd else (ya_ref, yb_ref)
            ghost[384:448, :] = ylo[...]
            ghost[448:, :] = yhi[...]

    sums = [None] * 3
    for ez in range(TZ):
        lanes = slice(ez * 512, (ez + 1) * 512)
        high, low = slot_columns(o_ref, ez)
        ends, middle = (
            jnp.dot(
                slot_onehot(pick(high), pick(low), first, 8),
                ghost[(first - 4) * 128 :, lanes],
                preferred_element_type=F32,
            )
            for pick, first in ((end_rows, 4), (middle_rows, 7))
        )
        count = 224
        both = jnp.concatenate(
            [
                ends[:128], middle[:count], ends[128:288],
                ends[288:416], middle[count:], ends[416:],
            ],
            axis=0,
        )
        resid = (t_ref[:, lanes] - blend(both, w_ref[:, lanes])).astype(BF16)
        for c in range(3):
            part = jnp.dot(
                mg_ref[c, :, lanes] * resid, table_ref[lanes, :], preferred_element_type=F32
            )
            sums[c] = part if ez == 0 else sums[c] + part
    for c in range(3):
        part = jnp.transpose(sums[c], (1, 0))
        l_ref[c * 32 : (c + 1) * 32, :] = part[:32] + part[32:64]
    choice = onehot(lane_map(maps_ref, "l_ysend"), ROWS)
    loads = l_ref[...]
    top = loads.astype(BF16)
    rest = (loads - top.astype(F32)).astype(BF16)
    msg_ref[...] = jnp.dot(
        jnp.concatenate([top, rest], axis=0), choice, preferred_element_type=F32
    ).astype(BF16)


def powers_kernel(
    flags_ref, lown_ref, ha_ref, hb_ref, la_ref, lb_ref, hchoice_ref, lchoice_ref, maps_ref, ochoice_ref,
    hown_ref, v_ref, dots_ref, h_ref, us, fs,
):
    row = lax.broadcasted_iota(jnp.int32, (8, GRID), 0)
    beyond_x = (lane_map(maps_ref, "x") >= TX) & (flags_ref[0] == 1)
    beyond_y = (lane_map(maps_ref, "y") >= TY) & (flags_ref[1] == 1)
    live = jnp.where(beyond_x | beyond_y, 0.0, 1.0)

    def scatter(f):
        out = []
        for c in range(3):
            sums = []
            for l in range(2):
                both = f(0, l, c) + pltpu.roll(f(1, l, c), 1, axis=1)
                split = jnp.where(row < 4, both, pltpu.roll(both, PITCH, axis=1))
                sums.append(split + pltpu.roll(split, 4, axis=0))
            a, b = sums
            lower = a + jnp.where((row & 3) == 0, 0.0, pltpu.roll(b, 1, axis=0))
            upper = b + jnp.where((row & 3) == 3, 0.0, pltpu.roll(a, 7, axis=0))
            out.append((lower * live, upper * live))
        return out

    def apply(u):
        for i in range(2):
            for j in range(2):
                shift = i * PITCH + j
                for d in range(3):
                    for l in range(2):
                        value = u[d][l]
                        if shift:
                            value = pltpu.roll(value, GRID - shift, axis=1)
                        us[((i * 2 + j) * 3 + d) * 2 + l] = value

        def tile_step(tile, carry):
            lanes = pl.ds(pl.multiple_of(tile * 128, 128), 128)
            uu = [us[k, :, lanes] for k in range(24)]
            acc = {}
            for k, (c, d) in enumerate(PAIRS):
                for tj in range(3):
                    for tl in range(3):
                        for i in range(2):
                            at = k * HROWS + (tj * 3 + tl) * 12 + i * 4
                            h = h_ref[tile, at : at + 8, :]
                            for mj in range(2):
                                nj = tj - mj
                                if nj not in (0, 1):
                                    continue
                                for ml in range(2):
                                    nl = tl - ml
                                    if nl not in (0, 1):
                                        continue
                                    for out_c, in_d in {(c, d), (d, c)}:
                                        term = h * uu[((i * 2 + mj) * 3 + in_d) * 2 + ml]
                                        key = (nj * 2 + nl) * 3 + out_c
                                        acc[key] = term if key not in acc else acc[key] + term
            for key in range(12):
                fs[key, :, lanes] = acc[key] * SCALE
            return carry

        lax.fori_loop(0, GRID // 128, tile_step, 0, unroll=4)
        return scatter(lambda j, l, c: fs[(j * 2 + l) * 3 + c])

    xlo = either(flags_ref[2], hb_ref[...], ha_ref[...])
    xhi = either(flags_ref[2], ha_ref[...], hb_ref[...])
    placed = jnp.dot(xlo, hchoice_ref[:, :256], preferred_element_type=F32)
    for tile in range(2):
        h_ref[tile] = hown_ref[tile] + placed[:, tile * 128 : (tile + 1) * 128]
    h_ref[6] = hown_ref[6] + jnp.dot(
        xhi, hchoice_ref[:, 256:], preferred_element_type=F32
    )
    xlo = either(flags_ref[2], lb_ref[...], la_ref[...])
    xhi = either(flags_ref[2], la_ref[...], lb_ref[...])
    source = jnp.concatenate([xlo[:192], xlo[192:], xhi[:192]], axis=1)
    placed = jnp.dot(source, lchoice_ref[...], preferred_element_type=F32)
    loads = lown_ref[...] + placed[:96] + placed[96:]

    def load_rows(j, l, c):
        at = c * 32 + (j * 2 + l) * 8
        return loads[at : at + 8, :]

    vectors = [scatter(load_rows)]
    for _ in range(3):
        vectors.append(apply(vectors[-1]))
    pieces = []
    for vec in vectors:
        for lower, upper in vec:
            pieces.append(
                jnp.where(row < 4, lower, jnp.where(row == 4, pltpu.roll(upper, 1, axis=0), 0.0))
            )
    own = select_lanes(jnp.concatenate(pieces, axis=0), ochoice_ref[...], 3)
    v_ref[...] = own
    lane = lax.broadcasted_iota(jnp.int32, (1, 128), 1)
    dots = jnp.zeros((1, 128), F32)
    for k, (a, b) in enumerate(DOTS):
        product = own[a * 24 : a * 24 + 24] * own[b * 24 : b * 24 + 24]
        total = jnp.sum(jnp.sum(product, axis=0, keepdims=True), axis=1, keepdims=True)
        dots = jnp.where(lane == k, total, dots)
    dots_ref[...] = jnp.broadcast_to(dots, dots_ref.shape)


def combine_kernel(v_ref, dots_ref, x_ref, r_ref):
    total = jnp.sum(dots_ref[...], axis=0, keepdims=True)
    gram = {}
    for k, (a, b) in enumerate(DOTS):
        gram[(a, b)] = gram[(b, a)] = total[:, k : k + 1]

    def inner(p, q):
        out = None
        for a, pa in p.items():
            for b, qb in q.items():
                term = pa * qb * gram[(a, b)]
                out = term if out is None else out + term
        return out

    def add(p, q, factor):
        out = dict(p)
        for a, qa in q.items():
            term = factor * qa
            out[a] = out[a] + term if a in out else term
        return out

    one = jnp.ones((1, 1), F32)
    increment, resid, direction = {}, {0: one}, {0: one}
    norm_now = gram[(0, 0)]
    for sweep in range(3):
        image = {}
        for a, pa in direction.items():
            image[a] = image[a] + TIKHONOV * pa if a in image else TIKHONOV * pa
            image[a + 1] = pa * (1.0 / SCALE)
        step_size = norm_now / inner(direction, image)
        increment = add(increment, direction, step_size)
        resid = add(resid, image, -step_size)
        if sweep < 2:
            norm_next = inner(resid, resid)
            direction = add(resid, direction, norm_next / norm_now)
            norm_now = norm_next
    at_x = lax.broadcasted_iota(jnp.int32, (TX, ROWS), 1) >> 5 == lax.broadcasted_iota(
        jnp.int32, (TX, ROWS), 0
    )
    at_y = lax.broadcasted_iota(jnp.int32, (ROWS, TY), 0) & 31 == lax.broadcasted_iota(
        jnp.int32, (ROWS, TY), 1
    )
    pieces = []
    for coefs in (increment, resid):
        for c in range(3):
            out = None
            for k, coef in coefs.items():
                at = (k * 3 + c) * 8
                term = coef * v_ref[at : at + 8, :]
                out = term if out is None else out + term
            for z in range(TZ + 1):
                pieces.append(jnp.where(at_x, out[z : z + 1, :], 0.0))
    split = select_lanes(
        jnp.concatenate(pieces, axis=0), jnp.where(at_y, 1.0, 0.0).astype(BF16), 3
    )
    half = 3 * (TZ + 1) * TX
    x_ref[...] = split[:half]
    r_ref[...] = split[half:]


def whole(shape):
    return pl.BlockSpec(shape, lambda *_: (0,) * len(shape))


def call(kernel, outs, *args, name, us, scratch=(), vmem=8, flags=None):
    operands = args if flags is None else (flags, *args)
    scalars = [] if flags is None else [pl.BlockSpec(memory_space=pltpu.SMEM)]
    return pl.pallas_call(
        kernel,
        out_shape=outs,
        in_specs=scalars + [pl.BlockSpec(memory_space=pltpu.VMEM)] * len(args),
        out_specs=jax.tree.map(lambda _: pl.BlockSpec(memory_space=pltpu.VMEM), outs),
        scratch_shapes=scratch,
        compiler_params=pltpu.CompilerParams(vmem_limit_bytes=vmem * 2**20),
        cost_estimate=cost(us),
        name=name,
    )(*operands)


def struct(*shape, dtype=F32):
    return jax.ShapeDtypeStruct(shape, dtype)


def cost(us):
    return pl.CostEstimate(flops=int(us * 1.1e9), transcendentals=0, bytes_accessed=0)


def swapped(value, axis, first):
    size = lax.axis_size(axis)
    pairs = []
    for low in range(1 if first else 0, size - 1, 2):
        pairs += [(low, low + 1), (low + 1, low)]
    return lax.ppermute(value, axis, pairs)


def per_device(
    reference_scan, ref_gradient, deformed_scan, interp_weights, sample_mask, block_list, offsets
):
    scan = reference_scan.reshape(ROWS, COL)
    grad = ref_gradient.reshape(3, ROWS, COL)
    weights = interp_weights.reshape(ROWS, COL)
    mask = sample_mask.reshape(ROWS, COL)
    moved = deformed_scan.reshape(ROWS, COL)
    moves = jnp.transpose(offsets, (0, 1, 3, 2))
    maps = jnp.asarray(lane_maps())
    lanes = lambda rows: pl.BlockSpec((rows, 512), lambda i: (0, i))
    params = pltpu.CompilerParams(vmem_limit_bytes=8 * 2**20)
    bf = functools.partial(struct, dtype=BF16)

    vmem = pl.BlockSpec(memory_space=pltpu.VMEM)
    at_x, at_y = lax.axis_index("gx"), lax.axis_index("gy")
    flags = jnp.stack(
        [
            at_x == lax.axis_size("gx") - 1,
            at_y == lax.axis_size("gy") - 1,
            at_x % 2 == 1,
            at_y % 2 == 1,
        ]
    ).astype(jnp.int32)
    xa, xb, ya, yb = pl.pallas_call(
        pack_kernel,
        out_shape=(bf(5, TY // 8, 8, COL), bf(5, TY // 8, 8, COL), bf(64, COL), bf(64, COL)),
        in_specs=[pl.BlockSpec(memory_space=pltpu.SMEM), pl.BlockSpec(memory_space=pltpu.HBM)],
        out_specs=(vmem,) * 4,
        scratch_shapes=[
            pltpu.VMEM((2, TX, 1, 8, COL), BF16),
            pltpu.SemaphoreType.DMA((4,)),
        ],
        compiler_params=params,
        cost_estimate=cost(8),
        name="pack",
    )(flags, deformed_scan.reshape(TX, TY // 8, 8, COL))
    xa = swapped(xa.reshape(160, COL), "gx", True)
    xb = swapped(xb.reshape(160, COL), "gx", False)
    moves, ya = lax.optimization_barrier((moves, ya))
    ya, yb = swapped(ya, "gy", True), swapped(yb, "gy", False)
    partial_image, after = call(
        own_samples_kernel, (struct(ROWS, COL), struct(8, 128)), scan, weights, moved, moves,
        name="own_samples", us=2, vmem=14,
    )
    ca, cb = call(
        corner_kernel, (bf(48, COL), bf(48, COL)), ya, yb, after, name="corners", us=1,
        flags=flags,
    )
    maps_late, ca = lax.optimization_barrier((maps, ca))
    ca, cb = swapped(ca, "gx", True), swapped(cb, "gx", False)

    coefs, coefs_y, coefs_x, masked = call(
        hessian_kernel,
        (bf(CROWS, ROWS), bf(CROWS, 128), bf(CROWS, 256), bf(3, ROWS, COL)),
        grad, mask, jnp.asarray(hessian_table()), maps_late,
        name="hessian", us=1,
    )
    ya_h, yb_h = swapped(coefs_y, "gy", True), swapped(coefs_y, "gy", False)
    loads, message = call(
        warp_kernel,
        (struct(96, ROWS), bf(192, 128)),
        partial_image, weights, masked, xa, xb, ca, cb, ya, yb, moves,
        jnp.asarray(load_table()), maps,
        name="warp", us=6, vmem=14, flags=flags, scratch=[pltpu.VMEM((512, COL), BF16)],
    )
    ytile_h, ha, hb = call(
        hessian_edge_kernel, (bf(CROWS, 128),) * 3, coefs_x, ya_h, yb_h, maps,
        name="hessian_edges", us=1, flags=flags,
    )
    la, lb = swapped(message, "gy", True), swapped(message, "gy", False)
    ytile_l, la, lb = call(
        load_edge_kernel, (bf(192, 128), bf(384, 128), bf(384, 128)), loads, la, lb, maps,
        name="load_edges", us=1, flags=flags,
    )
    ghosts = (
        swapped(ha, "gx", True), swapped(hb, "gx", False),
        swapped(la, "gx", True), swapped(lb, "gx", False),
    )
    stiffness, loads_grid, *choices = call(
        grid_kernel,
        (
            struct(GRID // 128, CROWS, 128), struct(96, GRID),
            bf(128, 384), bf(384, GRID), bf(GRID, ROWS),
        ),
        coefs, loads, ytile_h, ytile_l, maps,
        name="grid", us=3,
    )

    devices = lax.axis_size("gx") * lax.axis_size("gy")
    vectors, dots, _ = pl.pallas_call(
        powers_kernel,
        out_shape=(struct(96, ROWS), struct(devices, 128), struct(GRID // 128, CROWS, 128)),
        in_specs=[pl.BlockSpec(memory_space=pltpu.SMEM)] + [vmem] * 10,
        out_specs=(vmem,) * 3,
        scratch_shapes=[pltpu.VMEM((24, 8, GRID), F32), pltpu.VMEM((12, 8, GRID), F32)],
        input_output_aliases={10: 2},
        compiler_params=params,
        cost_estimate=cost(6),
        name="powers",
    )(
        flags, loads_grid, *ghosts, choices[0], choices[1], maps, choices[2],
        stiffness,
    )
    dots = lax.all_to_all(dots, ("gx", "gy"), 0, 0, tiled=True)
    increment, resid = call(
        combine_kernel, (struct(240, TY), struct(240, TY)), vectors, dots, name="combine", us=3
    )
    return tuple(
        jnp.transpose(out.reshape(3, TZ + 1, TX, TY), (0, 2, 3, 1)) for out in (increment, resid)
    )


def solution(mesh):
    return jax.shard_map(
        per_device,
        mesh=mesh,
        in_specs=(
            P("gx", "gy", None),
            P(None, "gx", "gy", None),
            P("gx", "gy", None),
            P("gx", "gy", None),
            P("gx", "gy", None),
            P("gx", "gy"),
            P(None, "gx", "gy", None),
        ),
        out_specs=(P(None, "gx", "gy", None), P(None, "gx", "gy", None)),
        check_vma=False,
    )
```

```python
import functools

import numpy as np

import jax
import jax.numpy as jnp
from jax import lax
from jax.experimental import pallas as pl
from jax.experimental.pallas import tpu as pltpu
from jax.sharding import PartitionSpec as P

F32 = jnp.float32
BF16 = jnp.bfloat16
TX, TY, TZ = 16, 32, 4
ROWS = TX * TY
COL = TZ * 512
PITCH = 40
GRID = 1024
HROWS = 112
CROWS = 6 * HROWS
TIKHONOV = 8.0
SCALE = 2.0**-8
PAIRS = [(0, 0), (0, 1), (0, 2), (1, 1), (1, 2), (2, 2)]
DOTS = [(0, 0), (0, 1), (0, 2), (0, 3), (1, 1), (1, 2), (1, 3), (2, 2), (2, 3)]


def voxel_factors():
    v = np.arange(512)
    coords = [(v // 64 + 0.5) / 8.0, (v // 8 % 8 + 0.5) / 8.0, (v % 8 + 0.5) / 8.0]
    return [(1.0 - t, t) for t in coords]


def hessian_table():
    s = voxel_factors()
    q = [(a * a, a * b, b * b) for a, b in s]
    table = np.zeros((HROWS, TZ, 512))
    for tj in range(3):
        for tl in range(3):
            for ti in range(3):
                t = (tj * 3 + tl) * 3 + ti
                for ez in range(TZ):
                    table[4 * t + ez, ez] = q[0][ti] * q[1][tj] * q[2][tl]
    table = np.concatenate([table, np.zeros((128 - HROWS, TZ, 512))])
    return np.ascontiguousarray(table.reshape(128, COL).T).astype(jnp.bfloat16)


def load_table():
    s = voxel_factors()
    table = np.zeros((32, TZ, 512), np.float32)
    for j in range(2):
        for l in range(2):
            for i in range(2):
                for ez in range(TZ):
                    table[(j * 2 + l) * 8 + i * 4 + ez, ez] = s[0][i] * s[1][j] * s[2][l]
    table = table.reshape(32, COL)
    high = table.astype(jnp.bfloat16)
    low = (table - high.astype(np.float32)).astype(jnp.bfloat16)
    both = np.concatenate([high, low, np.zeros((64, COL), high.dtype)], axis=0)
    return np.ascontiguousarray(both.T)


def edge_maps(low, high, xlo_lanes, xhi_lanes):
    ysend, ycoord = [], []
    for x in range(TX):
        for k in range(low):
            ysend.append(x * TY + TY - low + k)
            ycoord.append((x, k - low))
    for x in range(TX):
        for k in range(high):
            ysend.append(x * TY + k)
            ycoord.append((x, TY + k))
    lane_of = {c: n for n, c in enumerate(ycoord)}

    def strip(first, count, base):
        lanes, coord = [], []
        for x in range(first, first + count):
            for y in range(TY):
                lanes.append(x * TY + y)
                coord.append((x + base, y))
        for ys in (range(-low, 0), range(TY, TY + high)):
            for x in range(first, first + count):
                for y in ys:
                    lanes.append(ROWS + lane_of[(x, y)])
                    coord.append((x + base, y))
        return lanes, coord

    up, up_coord = strip(TX - low, low, -TX)
    up_lanes = list(range(len(up)))
    down, down_coord = strip(0, high, TX)
    source = {}
    for x in range(TX):
        for y in range(TY):
            source[(x, y)] = x * TY + y
    for n, c in enumerate(ycoord):
        source[c] = ROWS + n
    for n, c in zip(up_lanes, up_coord):
        source[c] = ROWS + 128 + n
    for n, c in enumerate(down_coord):
        source[c] = ROWS + 128 + xlo_lanes + n
    grid = np.full((GRID,), -1)
    for (x, y), lane in source.items():
        grid[(x + 4) * PITCH + y + 4] = lane

    def row(values, lanes):
        out = np.full((1, lanes), -1, np.int32)
        out[0, : len(values)] = values
        return out

    sent = np.full((1, xlo_lanes), -1, np.int32)
    sent[0, up_lanes] = up
    xsend = np.concatenate([sent, row(down, xhi_lanes)], axis=1)
    return row(ysend, 128), xsend, row(list(grid), GRID), low * TX


H_YSEND, H_XSEND, H_GRID, H_YLOW = edge_maps(3, 2, 128, 128)
L_YSEND, L_XSEND, L_GRID, L_YLOW = edge_maps(4, 3, 256, 128)
OWN_MAP = np.array(
    [[(x + 4) * PITCH + y + 4 for x in range(TX) for y in range(TY)]], np.int32
)


def lane_maps():
    position = np.arange(GRID)
    rows = np.full((8, GRID), -1, np.int32)
    rows[0] = H_GRID
    rows[1] = L_GRID
    rows[2] = position // PITCH - 4
    rows[3] = position % PITCH - 4
    rows[4, :512] = OWN_MAP
    rows[5, :128] = H_YSEND
    rows[5, 128:384] = np.where(H_XSEND < ROWS, H_XSEND, -1)
    rows[5, 384:640] = H_XSEND
    rows[6, :128] = L_YSEND
    rows[6, 128:512] = L_XSEND
    return rows


MAP = {
    "h_grid": (0, 0, 1024),
    "l_grid": (1, 0, 1024),
    "x": (2, 0, 1024),
    "y": (3, 0, 1024),
    "own": (4, 0, 512),
    "h_ysend": (5, 0, 128),
    "h_xown": (5, 128, 384),
    "h_xsend": (5, 384, 640),
    "l_ysend": (6, 0, 128),
    "l_xsend": (6, 128, 512),
}


def lane_map(maps_ref, name):
    row, first, last = MAP[name]
    return maps_ref[row : row + 1, first:last]


def onehot(index_row, depth):
    lanes = index_row.shape[1]
    rows = lax.broadcasted_iota(jnp.int32, (depth, lanes), 0)
    return jnp.where(rows == index_row, 1.0, 0.0).astype(BF16)


def select_lanes(value, choice, parts):
    pieces, rest = [], value
    for part in range(parts):
        pieces.append(rest.astype(BF16))
        rest = rest - pieces[-1].astype(F32)
    stacked = jnp.dot(jnp.concatenate(pieces, axis=0), choice, preferred_element_type=F32)
    rows = value.shape[0]
    total = stacked[:rows]
    for part in range(1, parts):
        total = total + stacked[part * rows : (part + 1) * rows]
    return total


def run_copies(sems, *moves):
    copies = [
        pltpu.make_async_copy(source, target, sems.at[k])
        for k, (source, target) in enumerate(moves)
    ]
    for copy in copies:
        copy.start()
    return copies


def either(flag, yes, no):
    return jnp.where(jnp.full(yes.shape, flag, jnp.int32) == 1, yes, no)


def pack_kernel(flags_ref, d_ref, xa_ref, xb_ref, ya_ref, yb_ref, ends, sems):
    odd_x, odd_y = flags_ref[2], flags_ref[3]
    high = TX - 5
    copies = run_copies(
        sems,
        (d_ref.at[pl.ds(0, TX), pl.ds(TY // 8 - 1, 1)], ends.at[0]),
        (d_ref.at[pl.ds(0, TX), pl.ds(0, 1)], ends.at[1]),
        (d_ref.at[pl.ds(high * odd_x, 5)], xa_ref),
        (d_ref.at[pl.ds(high - high * odd_x, 5)], xb_ref),
    )
    row = lax.broadcasted_iota(jnp.int32, (64, 128), 0)
    pos = lax.broadcasted_iota(jnp.int32, (64, 128), 1)
    found = []
    for k, at in enumerate((4, 0)):
        choice = jnp.where(pos == (row >> 2) * 8 + (row & 3) + at, 1.0, 0.0).astype(BF16)
        copies[k].wait()
        rows = ends[k].astype(F32).reshape(TX * 8, COL).astype(BF16)
        found.append(jnp.dot(choice, rows, preferred_element_type=F32))
    last, first = found
    ya_ref[...] = either(odd_y, last, first).astype(BF16)
    yb_ref[...] = either(odd_y, first, last).astype(BF16)
    copies[2].wait()
    copies[3].wait()


def corner_kernel(flags_ref, ya_ref, yb_ref, after_ref, a_ref, b_ref):
    for odd_x in range(2):
        for odd_y in range(2):

            @pl.when((flags_ref[2] == odd_x) & (flags_ref[3] == odd_y))
            def _():
                low, high = (yb_ref, ya_ref) if odd_y else (ya_ref, yb_ref)
                up, down = (a_ref, b_ref) if odd_x else (b_ref, a_ref)
                up[:24, :] = low[40:, :]
                up[24:, :] = high[40:, :]
                down[:24, :] = low[:24, :]
                down[24:, :] = high[:24, :]


def hessian_kernel(g_ref, m_ref, table_ref, maps_ref, c_ref, cy_ref, cx_ref, mg_ref):
    chunk = 256

    def step(i, carry):
        rows = pl.ds(pl.multiple_of(i * chunk, chunk), chunk)
        mask = m_ref[rows, :].astype(F32).astype(BF16)
        for c in range(3):
            mg_ref[c, rows, :] = g_ref[c, rows, :] * mask
        for k, (c, d) in enumerate(PAIRS):
            x = mg_ref[c, rows, :] * g_ref[d, rows, :]
            sums = jnp.dot(x, table_ref[...], preferred_element_type=F32)
            c_ref[k * HROWS : (k + 1) * HROWS, rows] = jnp.transpose(sums, (1, 0))[:HROWS].astype(BF16)
        return carry

    lax.fori_loop(0, ROWS // chunk, step, 0)
    for name, ref in (("h_ysend", cy_ref), ("h_xown", cx_ref)):
        choice = onehot(lane_map(maps_ref, name), ROWS)
        ref[...] = jnp.dot(c_ref[...], choice, preferred_element_type=F32).astype(BF16)


def y_tile(flags_ref, a_ref, b_ref, ylow):
    lane = lax.broadcasted_iota(jnp.int32, (1, 128), 1)
    odd_y = jnp.full((1, 128), flags_ref[3], jnp.int32) == 1
    return jnp.where((lane < ylow) != odd_y, a_ref[...], b_ref[...])


def store_pair(flags_ref, up, down, a_ref, b_ref):
    @pl.when(flags_ref[2] == 1)
    def _():
        a_ref[...] = up
        b_ref[...] = down

    @pl.when(flags_ref[2] == 0)
    def _():
        a_ref[...] = down
        b_ref[...] = up


def hessian_edge_kernel(flags_ref, cx_ref, ya_ref, yb_ref, maps_ref, y_ref, a_ref, b_ref):
    ytile = y_tile(flags_ref, ya_ref, yb_ref, H_YLOW)
    y_ref[...] = ytile
    choice = onehot(lane_map(maps_ref, "h_xsend") - ROWS, 128)
    sent = jnp.dot(ytile, choice, preferred_element_type=F32).astype(BF16) + cx_ref[...]
    store_pair(flags_ref, sent[:, :128], sent[:, 128:], a_ref, b_ref)


def load_edge_kernel(flags_ref, l_ref, ya_ref, yb_ref, maps_ref, y_ref, a_ref, b_ref):
    ytile = y_tile(flags_ref, ya_ref, yb_ref, L_YLOW)
    y_ref[...] = ytile
    high = l_ref[...].astype(BF16)
    low = (l_ref[...] - high.astype(F32)).astype(BF16)
    source = jnp.concatenate([jnp.concatenate([high, low], axis=0), ytile], axis=1)
    sent = jnp.dot(
        source, onehot(lane_map(maps_ref, "l_xsend"), ROWS + 128), preferred_element_type=F32
    ).astype(BF16)
    up = jnp.concatenate([sent[:, :128], sent[:, 128:256]], axis=0)
    down = jnp.concatenate([sent[:, 256:], jnp.zeros((192, 128), BF16)], axis=0)
    store_pair(flags_ref, up, down, a_ref, b_ref)


def own_grid_kernel(own_ref, maps_ref, out_ref, hchoice_ref, lchoice_ref, ochoice_ref):
    h_map, l_map = lane_map(maps_ref, "h_grid"), lane_map(maps_ref, "l_grid")
    placed = jnp.dot(own_ref[...], onehot(h_map, ROWS), preferred_element_type=F32)
    for tile in range(GRID // 128):
        out_ref[tile] = placed[:, tile * 128 : (tile + 1) * 128]
    hchoice_ref[:, :256] = onehot(h_map[:, :256] - (ROWS + 128), 128)
    hchoice_ref[:, 256:] = onehot(h_map[:, 768:896] - (ROWS + 256), 128)
    lchoice_ref[...] = onehot(l_map - (ROWS + 128), 384)
    ochoice_ref[...] = onehot(lane_map(maps_ref, "own"), GRID)


def grid_kernel(h_ref, l_ref, yh_ref, yl_ref, maps_ref, out_ref, lout_ref):
    choice = onehot(lane_map(maps_ref, "h_grid") - ROWS, 128)
    placed = jnp.dot(yh_ref[...], choice, preferred_element_type=F32)
    for tile in range(GRID // 128):
        out_ref[tile] = h_ref[tile] + placed[:, tile * 128 : (tile + 1) * 128]
    top = l_ref[...].astype(BF16)
    rest = (l_ref[...] - top.astype(F32)).astype(BF16)
    source = jnp.concatenate([jnp.concatenate([top, rest], axis=0), yl_ref[...]], axis=1)
    choice = onehot(lane_map(maps_ref, "l_grid"), ROWS + 128)
    placed = jnp.dot(source, choice, preferred_element_type=F32)
    lout_ref[...] = placed[:96] + placed[96:]


def sample_slot(x, y):
    ymid = (y >= 0) & (y < TY)
    ylo = y < 0
    xmid = (x >= 0) & (x < TX)
    xlo = x < 0
    mid = jnp.where(
        xmid, x * TY + y, jnp.where(xlo, 512 + (x + 4) * TY + y, 688 + (x - TX) * TY + y)
    )
    left = jnp.where(xmid, 896 + x * 4, jnp.where(xlo, 648 + (x + 4) * 4, 848 + (x - TX) * 4))
    right = jnp.where(xmid, 960 + x * 4, jnp.where(xlo, 672 + (x + 4) * 4, 872 + (x - TX) * 4))
    return jnp.where(ymid, mid, jnp.where(ylo, left + y + 4, right + y - TY))


def slot_columns(o_ref, ez):
    layer = lax.broadcasted_iota(jnp.int32, (TX, TZ, TY), 1) == ez
    ox, oy = (jnp.sum(jnp.where(layer, o_ref[axis], 0), axis=1) for axis in range(2))
    x = lax.broadcasted_iota(jnp.int32, (TX, TY), 0) + ox
    y = lax.broadcasted_iota(jnp.int32, (TX, TY), 1) + oy
    near, far = sample_slot(x, y), sample_slot(x + 1, y)
    parts = jnp.concatenate([near >> 7, near & 127, far >> 7, far & 127], axis=1)
    row = lax.broadcasted_iota(jnp.int32, (ROWS, TX), 0)
    col = lax.broadcasted_iota(jnp.int32, (ROWS, TX), 1)
    spread = jnp.dot(
        jnp.where(row >> 5 == col, 1.0, 0.0).astype(BF16),
        parts.astype(F32).astype(BF16),
        preferred_element_type=F32,
    )
    row = lax.broadcasted_iota(jnp.int32, (ROWS, 128), 0)
    col = lax.broadcasted_iota(jnp.int32, (ROWS, 128), 1)
    spread = jnp.where(row & 31 == col & 31, spread, 0.0).astype(BF16)
    row = lax.broadcasted_iota(jnp.int32, (128, 512), 0)
    col = lax.broadcasted_iota(jnp.int32, (128, 512), 1)
    ones = jnp.where(row >> 5 == col >> 7, 1.0, 0.0).astype(BF16)
    out = jnp.dot(spread, ones, preferred_element_type=F32).astype(BF16)
    high = jnp.concatenate([out[:, :128], out[:, 256:384]], axis=0)
    low = jnp.concatenate([out[:, 128:256], out[:, 384:]], axis=0)
    return high, low


def slot_onehot(high, low, first, last):
    lane = lax.broadcasted_iota(jnp.int32, low.shape, 1).astype(F32).astype(BF16)
    zero = jnp.zeros(low.shape, BF16)
    hit = jnp.where(low == lane, jnp.ones(low.shape, BF16), zero)
    return jnp.concatenate([jnp.where(high == float(first + k), hit, zero) for k in range(last - first)], axis=1)


def end_rows(value):
    return jnp.concatenate([value[:128], value[352:640], value[864:]], axis=0)


def middle_rows(value):
    return jnp.concatenate([value[128:352], value[640:864]], axis=0)


def blend(both, w):
    w = w.astype(F32)
    return w * both[:ROWS] + (1.0 - w) * both[ROWS:]


def own_samples_kernel(s_ref, w_ref, d_ref, o_ref, out_ref, after_ref):
    after_ref[...] = jnp.zeros_like(after_ref)
    for ez in range(TZ):
        lanes = slice(ez * 512, (ez + 1) * 512)
        high, low = slot_columns(o_ref, ez)
        both = jnp.dot(
            slot_onehot(high, low, 0, 4), d_ref[:, lanes], preferred_element_type=F32
        )
        out_ref[:, lanes] = s_ref[:, lanes].astype(F32) - blend(both, w_ref[:, lanes])


def warp_kernel(
    flags_ref, t_ref, w_ref, mg_ref, xa_ref, xb_ref, ca_ref, cb_ref, ya_ref, yb_ref, o_ref,
    table_ref, maps_ref,
    l_ref, msg_ref, ghost,
):
    for odd in range(2):

        @pl.when(flags_ref[2] == odd)
        def _():
            xlo, xhi = (xb_ref, xa_ref) if odd else (xa_ref, xb_ref)
            clo, chi = (cb_ref, ca_ref) if odd else (ca_ref, cb_ref)
            ghost[:128, :] = xlo[32:, :]
            ghost[128:176, :] = clo[...]
            ghost[176:336, :] = xhi[...]
            ghost[336:384, :] = chi[...]

        @pl.when(flags_ref[3] == odd)
        def _():
            ylo, yhi = (yb_ref, ya_ref) if odd else (ya_ref, yb_ref)
            ghost[384:448, :] = ylo[...]
            ghost[448:, :] = yhi[...]

    sums = [None] * 3
    for ez in range(TZ):
        lanes = slice(ez * 512, (ez + 1) * 512)
        high, low = slot_columns(o_ref, ez)
        ends, middle = (
            jnp.dot(
                slot_onehot(pick(high), pick(low), first, 8),
                ghost[(first - 4) * 128 :, lanes],
                preferred_element_type=F32,
            )
            for pick, first in ((end_rows, 4), (middle_rows, 7))
        )
        count = 224
        both = jnp.concatenate(
            [
                ends[:128], middle[:count], ends[128:288],
                ends[288:416], middle[count:], ends[416:],
            ],
            axis=0,
        )
        resid = (t_ref[:, lanes] - blend(both, w_ref[:, lanes])).astype(BF16)
        for c in range(3):
            part = jnp.dot(
                mg_ref[c, :, lanes] * resid, table_ref[lanes, :], preferred_element_type=F32
            )
            sums[c] = part if ez == 0 else sums[c] + part
    for c in range(3):
        part = jnp.transpose(sums[c], (1, 0))
        l_ref[c * 32 : (c + 1) * 32, :] = part[:32] + part[32:64]
    choice = onehot(lane_map(maps_ref, "l_ysend"), ROWS)
    loads = l_ref[...]
    top = loads.astype(BF16)
    rest = (loads - top.astype(F32)).astype(BF16)
    msg_ref[...] = jnp.dot(
        jnp.concatenate([top, rest], axis=0), choice, preferred_element_type=F32
    ).astype(BF16)


def powers_kernel(
    flags_ref, lown_ref, ha_ref, hb_ref, la_ref, lb_ref, hchoice_ref, lchoice_ref, maps_ref, ochoice_ref,
    hown_ref, v_ref, dots_ref, h_ref, us, fs,
):
    row = lax.broadcasted_iota(jnp.int32, (8, GRID), 0)
    beyond_x = (lane_map(maps_ref, "x") >= TX) & (flags_ref[0] == 1)
    beyond_y = (lane_map(maps_ref, "y") >= TY) & (flags_ref[1] == 1)
    live = jnp.where(beyond_x | beyond_y, 0.0, 1.0)

    def scatter(f):
        out = []
        for c in range(3):
            sums = []
            for l in range(2):
                both = f(0, l, c) + pltpu.roll(f(1, l, c), 1, axis=1)
                split = jnp.where(row < 4, both, pltpu.roll(both, PITCH, axis=1))
                sums.append(split + pltpu.roll(split, 4, axis=0))
            a, b = sums
            lower = a + jnp.where((row & 3) == 0, 0.0, pltpu.roll(b, 1, axis=0))
            upper = b + jnp.where((row & 3) == 3, 0.0, pltpu.roll(a, 7, axis=0))
            out.append((lower * live, upper * live))
        return out

    def apply(u):
        for i in range(2):
            for j in range(2):
                shift = i * PITCH + j
                for d in range(3):
                    for l in range(2):
                        value = u[d][l]
                        if shift:
                            value = pltpu.roll(value, GRID - shift, axis=1)
                        us[((i * 2 + j) * 3 + d) * 2 + l] = value

        def tile_step(tile, carry):
            lanes = pl.ds(pl.multiple_of(tile * 128, 128), 128)
            uu = [us[k, :, lanes] for k in range(24)]
            acc = {}
            for k, (c, d) in enumerate(PAIRS):
                for tj in range(3):
                    for tl in range(3):
                        for i in range(2):
                            at = k * HROWS + (tj * 3 + tl) * 12 + i * 4
                            h = h_ref[tile, at : at + 8, :]
                            for mj in range(2):
                                nj = tj - mj
                                if nj not in (0, 1):
                                    continue
                                for ml in range(2):
                                    nl = tl - ml
                                    if nl not in (0, 1):
                                        continue
                                    for out_c, in_d in {(c, d), (d, c)}:
                                        term = h * uu[((i * 2 + mj) * 3 + in_d) * 2 + ml]
                                        key = (nj * 2 + nl) * 3 + out_c
                                        acc[key] = term if key not in acc else acc[key] + term
            for key in range(12):
                fs[key, :, lanes] = acc[key] * SCALE
            return carry

        lax.fori_loop(0, GRID // 128, tile_step, 0, unroll=4)
        return scatter(lambda j, l, c: fs[(j * 2 + l) * 3 + c])

    xlo = either(flags_ref[2], hb_ref[...], ha_ref[...])
    xhi = either(flags_ref[2], ha_ref[...], hb_ref[...])
    placed = jnp.dot(xlo, hchoice_ref[:, :256], preferred_element_type=F32)
    for tile in range(2):
        h_ref[tile] = hown_ref[tile] + placed[:, tile * 128 : (tile + 1) * 128]
    h_ref[6] = hown_ref[6] + jnp.dot(
        xhi, hchoice_ref[:, 256:], preferred_element_type=F32
    )
    xlo = either(flags_ref[2], lb_ref[...], la_ref[...])
    xhi = either(flags_ref[2], la_ref[...], lb_ref[...])
    source = jnp.concatenate([xlo[:192], xlo[192:], xhi[:192]], axis=1)
    placed = jnp.dot(source, lchoice_ref[...], preferred_element_type=F32)
    loads = lown_ref[...] + placed[:96] + placed[96:]

    def load_rows(j, l, c):
        at = c * 32 + (j * 2 + l) * 8
        return loads[at : at + 8, :]

    vectors = [scatter(load_rows)]
    for _ in range(3):
        vectors.append(apply(vectors[-1]))
    pieces = []
    for vec in vectors:
        for lower, upper in vec:
            pieces.append(
                jnp.where(row < 4, lower, jnp.where(row == 4, pltpu.roll(upper, 1, axis=0), 0.0))
            )
    own = select_lanes(jnp.concatenate(pieces, axis=0), ochoice_ref[...], 3)
    v_ref[...] = own
    lane = lax.broadcasted_iota(jnp.int32, (1, 128), 1)
    dots = jnp.zeros((1, 128), F32)
    for k, (a, b) in enumerate(DOTS):
        product = own[a * 24 : a * 24 + 24] * own[b * 24 : b * 24 + 24]
        total = jnp.sum(jnp.sum(product, axis=0, keepdims=True), axis=1, keepdims=True)
        dots = jnp.where(lane == k, total, dots)
    dots_ref[...] = jnp.broadcast_to(dots, dots_ref.shape)


def combine_kernel(v_ref, dots_ref, x_ref, r_ref):
    total = jnp.sum(dots_ref[...], axis=0, keepdims=True)
    gram = {}
    for k, (a, b) in enumerate(DOTS):
        gram[(a, b)] = gram[(b, a)] = total[:, k : k + 1]

    def inner(p, q):
        out = None
        for a, pa in p.items():
            for b, qb in q.items():
                term = pa * qb * gram[(a, b)]
                out = term if out is None else out + term
        return out

    def add(p, q, factor):
        out = dict(p)
        for a, qa in q.items():
            term = factor * qa
            out[a] = out[a] + term if a in out else term
        return out

    one = jnp.ones((1, 1), F32)
    increment, resid, direction = {}, {0: one}, {0: one}
    norm_now = gram[(0, 0)]
    for sweep in range(3):
        image = {}
        for a, pa in direction.items():
            image[a] = image[a] + TIKHONOV * pa if a in image else TIKHONOV * pa
            image[a + 1] = pa * (1.0 / SCALE)
        step_size = norm_now / inner(direction, image)
        increment = add(increment, direction, step_size)
        resid = add(resid, image, -step_size)
        if sweep < 2:
            norm_next = inner(resid, resid)
            direction = add(resid, direction, norm_next / norm_now)
            norm_now = norm_next
    at_x = lax.broadcasted_iota(jnp.int32, (TX, ROWS), 1) >> 5 == lax.broadcasted_iota(
        jnp.int32, (TX, ROWS), 0
    )
    at_y = lax.broadcasted_iota(jnp.int32, (ROWS, TY), 0) & 31 == lax.broadcasted_iota(
        jnp.int32, (ROWS, TY), 1
    )
    pieces = []
    for coefs in (increment, resid):
        for c in range(3):
            out = None
            for k, coef in coefs.items():
                at = (k * 3 + c) * 8
                term = coef * v_ref[at : at + 8, :]
                out = term if out is None else out + term
            for z in range(TZ + 1):
                pieces.append(jnp.where(at_x, out[z : z + 1, :], 0.0))
    split = select_lanes(
        jnp.concatenate(pieces, axis=0), jnp.where(at_y, 1.0, 0.0).astype(BF16), 3
    )
    half = 3 * (TZ + 1) * TX
    x_ref[...] = split[:half]
    r_ref[...] = split[half:]


def whole(shape):
    return pl.BlockSpec(shape, lambda *_: (0,) * len(shape))


def call(kernel, outs, *args, name, us, scratch=(), vmem=8, flags=None):
    operands = args if flags is None else (flags, *args)
    scalars = [] if flags is None else [pl.BlockSpec(memory_space=pltpu.SMEM)]
    return pl.pallas_call(
        kernel,
        out_shape=outs,
        in_specs=scalars + [pl.BlockSpec(memory_space=pltpu.VMEM)] * len(args),
        out_specs=jax.tree.map(lambda _: pl.BlockSpec(memory_space=pltpu.VMEM), outs),
        scratch_shapes=scratch,
        compiler_params=pltpu.CompilerParams(vmem_limit_bytes=vmem * 2**20),
        cost_estimate=cost(us),
        name=name,
    )(*operands)


def struct(*shape, dtype=F32):
    return jax.ShapeDtypeStruct(shape, dtype)


def cost(us):
    return pl.CostEstimate(flops=int(us * 1.1e9), transcendentals=0, bytes_accessed=0)


def swapped(value, axis, first):
    size = lax.axis_size(axis)
    pairs = []
    for low in range(1 if first else 0, size - 1, 2):
        pairs += [(low, low + 1), (low + 1, low)]
    return lax.ppermute(value, axis, pairs)


def per_device(
    reference_scan, ref_gradient, deformed_scan, interp_weights, sample_mask, block_list, offsets
):
    scan = reference_scan.reshape(ROWS, COL)
    grad = ref_gradient.reshape(3, ROWS, COL)
    weights = interp_weights.reshape(ROWS, COL)
    mask = sample_mask.reshape(ROWS, COL)
    moved = deformed_scan.reshape(ROWS, COL)
    moves = jnp.transpose(offsets, (0, 1, 3, 2))
    maps = jnp.asarray(lane_maps())
    lanes = lambda rows: pl.BlockSpec((rows, 512), lambda i: (0, i))
    params = pltpu.CompilerParams(vmem_limit_bytes=8 * 2**20)
    bf = functools.partial(struct, dtype=BF16)

    vmem = pl.BlockSpec(memory_space=pltpu.VMEM)
    at_x, at_y = lax.axis_index("gx"), lax.axis_index("gy")
    flags = jnp.stack(
        [
            at_x == lax.axis_size("gx") - 1,
            at_y == lax.axis_size("gy") - 1,
            at_x % 2 == 1,
            at_y % 2 == 1,
        ]
    ).astype(jnp.int32)
    xa, xb, ya, yb = pl.pallas_call(
        pack_kernel,
        out_shape=(bf(5, TY // 8, 8, COL), bf(5, TY // 8, 8, COL), bf(64, COL), bf(64, COL)),
        in_specs=[pl.BlockSpec(memory_space=pltpu.SMEM), pl.BlockSpec(memory_space=pltpu.HBM)],
        out_specs=(vmem,) * 4,
        scratch_shapes=[
            pltpu.VMEM((2, TX, 1, 8, COL), BF16),
            pltpu.SemaphoreType.DMA((4,)),
        ],
        compiler_params=params,
        cost_estimate=cost(8),
        name="pack",
    )(flags, deformed_scan.reshape(TX, TY // 8, 8, COL))
    xa = swapped(xa.reshape(160, COL), "gx", True)
    xb = swapped(xb.reshape(160, COL), "gx", False)
    moves, ya = lax.optimization_barrier((moves, ya))
    ya, yb = swapped(ya, "gy", True), swapped(yb, "gy", False)
    partial_image, after = call(
        own_samples_kernel, (struct(ROWS, COL), struct(8, 128)), scan, weights, moved, moves,
        name="own_samples", us=2, vmem=14,
    )
    ca, cb = call(
        corner_kernel, (bf(48, COL), bf(48, COL)), ya, yb, after, name="corners", us=1,
        flags=flags,
    )
    maps_late, ca = lax.optimization_barrier((maps, ca))
    ca, cb = swapped(ca, "gx", True), swapped(cb, "gx", False)

    coefs, coefs_y, coefs_x, masked = call(
        hessian_kernel,
        (bf(CROWS, ROWS), bf(CROWS, 128), bf(CROWS, 256), bf(3, ROWS, COL)),
        grad, mask, jnp.asarray(hessian_table()), maps_late,
        name="hessian", us=1,
    )
    stiffness, *choices = call(
        own_grid_kernel,
        (struct(GRID // 128, CROWS, 128), bf(128, 384), bf(384, GRID), bf(GRID, ROWS)),
        coefs, maps, name="own_grid", us=1,
    )
    moves, stiffness = lax.optimization_barrier((moves, stiffness))
    ya_h, yb_h = swapped(coefs_y, "gy", True), swapped(coefs_y, "gy", False)
    loads, message = call(
        warp_kernel,
        (struct(96, ROWS), bf(192, 128)),
        partial_image, weights, masked, xa, xb, ca, cb, ya, yb, moves,
        jnp.asarray(load_table()), maps,
        name="warp", us=6, vmem=14, flags=flags, scratch=[pltpu.VMEM((512, COL), BF16)],
    )
    ytile_h, ha, hb = call(
        hessian_edge_kernel, (bf(CROWS, 128),) * 3, coefs_x, ya_h, yb_h, maps,
        name="hessian_edges", us=1, flags=flags,
    )
    la, lb = swapped(message, "gy", True), swapped(message, "gy", False)
    ytile_l, la, lb = call(
        load_edge_kernel, (bf(192, 128), bf(384, 128), bf(384, 128)), loads, la, lb, maps,
        name="load_edges", us=1, flags=flags,
    )
    ghosts = (
        swapped(ha, "gx", True), swapped(hb, "gx", False),
        swapped(la, "gx", True), swapped(lb, "gx", False),
    )
    stiffness, loads_grid = call(
        grid_kernel, (struct(GRID // 128, CROWS, 128), struct(96, GRID)),
        stiffness, loads, ytile_h, ytile_l, maps,
        name="grid", us=1,
    )

    devices = lax.axis_size("gx") * lax.axis_size("gy")
    vectors, dots, _ = pl.pallas_call(
        powers_kernel,
        out_shape=(struct(96, ROWS), struct(devices, 128), struct(GRID // 128, CROWS, 128)),
        in_specs=[pl.BlockSpec(memory_space=pltpu.SMEM)] + [vmem] * 10,
        out_specs=(vmem,) * 3,
        scratch_shapes=[pltpu.VMEM((24, 8, GRID), F32), pltpu.VMEM((12, 8, GRID), F32)],
        input_output_aliases={10: 2},
        compiler_params=params,
        cost_estimate=cost(6),
        name="powers",
    )(
        flags, loads_grid, *ghosts, choices[0], choices[1], maps, choices[2],
        stiffness,
    )
    dots = lax.all_to_all(dots, ("gx", "gy"), 0, 0, tiled=True)
    increment, resid = call(
        combine_kernel, (struct(240, TY), struct(240, TY)), vectors, dots, name="combine", us=3
    )
    return tuple(
        jnp.transpose(out.reshape(3, TZ + 1, TX, TY), (0, 2, 3, 1)) for out in (increment, resid)
    )


def solution(mesh):
    return jax.shard_map(
        per_device,
        mesh=mesh,
        in_specs=(
            P("gx", "gy", None),
            P(None, "gx", "gy", None),
            P("gx", "gy", None),
            P("gx", "gy", None),
            P("gx", "gy", None),
            P("gx", "gy"),
            P(None, "gx", "gy", None),
        ),
        out_specs=(P(None, "gx", "gy", None), P(None, "gx", "gy", None)),
        check_vma=False,
    )
```
